512 devices in a mesh: gx: 16 (over z, core), gy: 8 (over y), gz: 4 (over x).
Axes of the slice: x: 4, y: 8, z: 8, core: 2. Of those that a mesh axis runs over, the one named last changes fastest.
Arguments:
- snapshot: float32 [512, 1280, 512], P('gx', 'gy', 'gz'), may hold values from -40 to 40
Outputs:
- basis: float32 [512, 128], P('gx')
- core: float32 [128, 1280, 512], P('gx', 'gy', 'gz')
The draws below stay inside these ranges and needn't reach their ends.
All inputs are finite; a program needn't handle non-finite values.
Results may differ from the reference program's by a relative error of at most 0.0002.
Values sent between devices are 32-bit elements; how exact they have to be, the bound alone decides.
A program may use at most 64 MiB of HBM per device.

```python
import jax
import jax.numpy as jnp
from jax import lax

NX = 512
RANK = 128
ITERS = 2
NY = 1280
NZ = 512


def draw_snapshot(key, part):
    key_left, key_right, key_noise = jax.random.split(key, 3)
    left = jax.random.normal(key_left, (NX, RANK), jnp.float32)
    right = jax.random.normal(key_right, (RANK, NY * NZ), jnp.float32)
    signal = jnp.dot(left, right, precision=lax.Precision.HIGHEST) / jnp.sqrt(jnp.float32(RANK))
    noise = jax.random.normal(key_noise, (NX, NY * NZ), jnp.float32)
    field = 3.0 * signal + noise
    return jnp.clip(field, -40.0, 40.0).reshape(NX, NY, NZ)


def setup_inputs(seed: int = 0) -> dict:
    splits = jax.random.split(jax.random.key(seed), 2)
    return {
        "snapshot": draw_snapshot(jax.random.fold_in(splits[1], 71), 0),
    }


def orthonormal(matrix):
    cross = jnp.dot(matrix.T.astype(jnp.float32), matrix.astype(jnp.float32), precision=lax.Precision.HIGHEST, preferred_element_type=jnp.float32)
    lower = jnp.linalg.cholesky(cross)
    return jax.scipy.linalg.solve_triangular(lower, matrix.T, lower=True).T

def reference(snapshot):
    unfold = snapshot.reshape(NX, NY * NZ)
    gram = jnp.dot(unfold.astype(jnp.float32), unfold.T.astype(jnp.float32), precision=lax.Precision.HIGHEST, preferred_element_type=jnp.float32)
    factor = jnp.linalg.cholesky(gram)
    basis = orthonormal(factor[:, :RANK])
    for step in range(ITERS):
        inner = jnp.dot(factor.T.astype(jnp.float32), basis.astype(jnp.float32), precision=lax.Precision.HIGHEST, preferred_element_type=jnp.float32)
        basis = orthonormal(jnp.dot(factor.astype(jnp.float32), inner.astype(jnp.float32), precision=lax.Precision.HIGHEST, preferred_element_type=jnp.float32))
    core = jnp.dot(basis.T.astype(jnp.float32), unfold.astype(jnp.float32), precision=lax.Precision.HIGHEST, preferred_element_type=jnp.float32)
    return (basis, core.reshape(RANK, NY, NZ))
```

```python
import functools

import jax
import jax.numpy as jnp
from jax import lax
from jax.experimental import pallas as pl
from jax.experimental.pallas import tpu as pltpu
from jax.sharding import PartitionSpec as P

RANK = 128
ITERS = 2
NX = 512
GX, GY, GZ = 16, 8, 4
MESH = pl.DeviceIdType.MESH
VMEM = pltpu.VMEM
BLOCK = 128
NB = NX // BLOCK
PAIRS = [(i, j) for j in range(NB) for i in range(j, NB)]
PLANE = GY * GZ
PIECE = 24
HALF = PLANE * PIECE
PACKED = 2 * HALF
GROUPS = 5


def split(x):
    hi = x.astype(jnp.bfloat16)
    lo = (x - hi.astype(jnp.float32)).astype(jnp.bfloat16)
    return hi, lo


def contract(a, b, ca, cb):
    return lax.dot_general(a, b, (((ca,), (cb,)), ((), ())), preferred_element_type=jnp.float32)


def dot_split(a, b, ca=1, cb=0):
    (ah, al), (bh, bl) = a, b
    return contract(ah, bh, ca, cb) + (contract(ah, bl, ca, cb) + contract(al, bh, ca, cb))


def gather_gram_kernel(snap_ref, fib_ref, packed_ref, acc_ref, half_ref, parts_ref, levels_ref, own_ref,
                       send_sem, fib_sem, core_send, core_recv, part_send, part_recv,
                       level_send, level_recv, piece_send, piece_recv, back_send, back_recv):
    gx, gy, gz = lax.axis_index("gx"), lax.axis_index("gy"), lax.axis_index("gz")
    z, core = gx // 2, gx % 2
    rows = snap_ref.shape[1]
    ycount = fib_ref.shape[0]
    per = ycount // GROUPS
    partner = 2 * z + (1 - core)
    peers = []
    for dz in (4, 3, 5, 2, 6, 1, 7):
        for flip in (0, 1):
            peers.append(lax.rem(z + dz, 8) * 2 + (core if flip == 0 else 1 - core))
    peers.append(partner)
    plane = [(dy, dx) for dy in range(GY) for dx in range(GZ) if (dy, dx) != (0, 0)]

    def across(dy, dx):
        return lax.rem(gy + dy, GY), lax.rem(gz + dx, GZ)

    barrier = pltpu.get_barrier_semaphore()
    for peer in peers:
        pl.semaphore_signal(barrier, inc=1, device_id={"gx": peer}, device_id_type=MESH)
    for dy, dx in plane:
        ty, tx = across(dy, dx)
        pl.semaphore_signal(barrier, inc=1, device_id={"gy": ty, "gz": tx}, device_id_type=MESH)
    pl.semaphore_wait(barrier, len(peers) + len(plane))

    place = pl.ds(pl.multiple_of(gx * rows, rows), rows)
    for g in range(GROUPS):
        here = pl.ds(g * per, per)
        pltpu.make_async_copy(
            snap_ref.at[pl.ds(gx * ycount + g * per, per)], fib_ref.at[here, place], fib_sem.at[g]
        ).start()
        for peer in peers:
            pltpu.make_async_remote_copy(
                src_ref=snap_ref.at[pl.ds(peer * ycount + g * per, per)],
                dst_ref=fib_ref.at[here, place],
                send_sem=send_sem,
                recv_sem=fib_sem.at[g],
                device_id={"gx": peer},
                device_id_type=MESH,
            ).start()

    acc_ref[...] = jnp.zeros_like(acc_ref)
    for g in range(GROUPS):
        here = fib_ref.at[pl.ds(g * per, per)]
        pltpu.make_async_copy(here, here, fib_sem.at[g]).wait()
        for y in range(per):
            blocks = [split(fib_ref[g * per + y, pl.ds(b * BLOCK, BLOCK), :]) for b in range(NB)]
            for n, (i, j) in enumerate(PAIRS):
                at = pl.ds(n * BLOCK, BLOCK)
                acc_ref[at, :] += dot_split(blocks[i], blocks[j], 1, 1)
    sent = snap_ref.at[pl.ds(0, 15 * ycount)]
    pltpu.make_async_copy(sent, sent, send_sem).wait()

    mine = pl.multiple_of(core * HALF, HALF)
    other = pl.multiple_of((1 - core) * HALF, HALF)
    swap = pltpu.make_async_remote_copy(
        src_ref=acc_ref.at[pl.ds(other, HALF)], dst_ref=half_ref,
        send_sem=core_send, recv_sem=core_recv, device_id={"gx": partner}, device_id_type=MESH)
    swap.start()
    swap.wait()
    half_ref[...] += acc_ref[pl.ds(mine, HALF), :]

    slot = gy * GZ + gz
    for dy, dx in plane:
        ty, tx = across(dy, dx)
        theirs = ty * GZ + tx
        pltpu.make_async_remote_copy(
            src_ref=half_ref.at[pl.ds(pl.multiple_of(theirs * PIECE, 8), PIECE)],
            dst_ref=parts_ref.at[dy * GZ + dx - 1],
            send_sem=part_send, recv_sem=part_recv,
            device_id={"gy": ty, "gz": tx}, device_id_type=MESH).start()
    pieces = half_ref.at[pl.ds(0, len(plane) * PIECE)]
    pltpu.make_async_copy(pieces, pieces, part_send).wait()
    pltpu.make_async_copy(parts_ref, parts_ref, part_recv).wait()
    total = half_ref[pl.ds(pl.multiple_of(slot * PIECE, 8), PIECE), :]
    for n in range(len(plane)):
        total = total + parts_ref[n]
    own_ref[...] = total

    for dz in range(1, 8):
        pltpu.make_async_remote_copy(
            src_ref=own_ref, dst_ref=levels_ref.at[dz - 1],
            send_sem=level_send, recv_sem=level_recv,
            device_id={"gx": lax.rem(z + dz, 8) * 2 + core}, device_id_type=MESH).start()
    pieces = half_ref.at[pl.ds(0, 7 * PIECE)]
    pltpu.make_async_copy(pieces, pieces, level_send).wait()
    pltpu.make_async_copy(levels_ref, levels_ref, level_recv).wait()
    total = own_ref[...]
    start = own_ref[...]
    for level in range(8):
        pick = start
        for dz in range(1, 8):
            pick = jnp.where(lax.rem(level + dz, 8) == z, levels_ref[dz - 1], pick)
        total = pick if level == 0 else total + pick
    at = pl.ds(pl.multiple_of(mine + slot * PIECE, 8), PIECE)
    own_ref[...] = total
    packed_ref[at, :] = total

    for dy, dx in plane:
        ty, tx = across(dy, dx)
        pltpu.make_async_remote_copy(
            src_ref=own_ref, dst_ref=packed_ref.at[at],
            send_sem=piece_send, recv_sem=piece_recv,
            device_id={"gy": ty, "gz": tx}, device_id_type=MESH).start()
    pltpu.make_async_copy(parts_ref, parts_ref, piece_send).wait()
    pltpu.make_async_copy(parts_ref, parts_ref, piece_recv).wait()
    swap = pltpu.make_async_remote_copy(
        src_ref=packed_ref.at[pl.ds(mine, HALF)], dst_ref=packed_ref.at[pl.ds(mine, HALF)],
        send_sem=back_send, recv_sem=back_recv, device_id={"gx": partner}, device_id_type=MESH)
    swap.start()
    swap.wait()


def gather_gram(snap):
    ycount = snap.shape[0] // GX
    dma = pltpu.SemaphoreType.DMA
    return pl.pallas_call(
        gather_gram_kernel,
        out_shape=(jax.ShapeDtypeStruct((ycount, NX, BLOCK), jnp.float32),
                   jax.ShapeDtypeStruct((PACKED, BLOCK), jnp.float32)),
        in_specs=[pl.BlockSpec(memory_space=pl.ANY)],
        out_specs=(pl.BlockSpec(memory_space=VMEM), pl.BlockSpec(memory_space=VMEM)),
        scratch_shapes=[
            VMEM((PACKED, BLOCK), jnp.float32),
            VMEM((HALF, BLOCK), jnp.float32),
            VMEM((PLANE - 1, PIECE, BLOCK), jnp.float32),
            VMEM((7, PIECE, BLOCK), jnp.float32),
            VMEM((PIECE, BLOCK), jnp.float32),
            dma, dma((GROUPS,)), dma, dma, dma, dma, dma, dma, dma, dma, dma, dma,
        ],
        compiler_params=pltpu.CompilerParams(collective_id=0, has_side_effects=True),
    )(snap)


def inverse_factor(a):
    n = a.shape[0]
    tiles = [a[8 * t:8 * t + 8, :] for t in range(n // 8)]
    lane = lax.broadcasted_iota(jnp.int32, (8, n), 1)
    sub = lax.broadcasted_iota(jnp.int32, (8, n), 0)
    out = []
    for p in range(n // 8):
        base = 8 * p
        own = tiles[p]
        cols = [jnp.broadcast_to(own[:, base + j:base + j + 1], (8, n)) for j in range(8)]
        s = [[jnp.broadcast_to(cols[j][i:i + 1, :], (8, n)) for j in range(i + 1)] for i in range(8)]
        panel = (lane >= base) & (lane < base + 8)
        rows = [jnp.broadcast_to(own[j:j + 1, :], (8, n)) for j in range(8)]
        rows = [jnp.where(lane == base + j, 1.0, jnp.where(panel, 0.0, rows[j])) for j in range(8)]
        rinv, low = [], [[None] * 8 for _ in range(8)]
        for j in range(8):
            r = 1.0 / s[j][j]
            rinv.append(r)
            for i in range(j + 1, 8):
                low[i][j] = s[i][j] * r
            for i in range(j + 1, 8):
                for k in range(j + 1, i + 1):
                    s[i][k] = s[i][k] - low[i][j] * s[k][j]
        for j in range(8):
            for i in range(j):
                rows[j] = rows[j] - low[j][i] * rows[i]
        scaled = rows[0] * jnp.sqrt(rinv[0])
        for j in range(1, 8):
            scaled = jnp.where(sub == j, rows[j] * jnp.sqrt(rinv[j]), scaled)
        out.append(jnp.where(lane <= sub + base, scaled, 0.0))
        for t in range(p + 1, n // 8):
            tile = tiles[t]
            c = [jnp.broadcast_to(tile[:, base + j:base + j + 1], (8, n)) for j in range(8)]
            acc = jnp.where(panel, 0.0, tile)
            for j in range(8):
                for i in range(j):
                    c[j] = c[j] - c[i] * low[j][i]
            for j in range(8):
                acc = acc - (c[j] * rinv[j]) * rows[j]
            tiles[t] = acc
    return jnp.concatenate(out, axis=0)


def orth(m):
    m = split(m)
    return dot_split(m, split(inverse_factor(dot_split(m, m, 0, 0))), 1, 1)


def basis_kernel(packed_ref, basis_ref):
    blocks = {}
    for n, (i, j) in enumerate(PAIRS):
        blocks[i, j] = packed_ref[pl.ds(n * BLOCK, BLOCK), :]
    for i, j in PAIRS:
        if i != j:
            blocks[j, i] = blocks[i, j].T
    columns = [jnp.concatenate([blocks[i, j] for i in range(NB)], axis=0) for j in range(NB)]
    basis = orth(columns[0])
    gram = split(jnp.concatenate(columns, axis=1))
    for step in range(ITERS):
        basis = orth(dot_split(gram, split(basis)))
    basis_ref[...] = basis


def make_basis(packed):
    return pl.pallas_call(
        basis_kernel,
        out_shape=jax.ShapeDtypeStruct((NX, RANK), jnp.float32),
        in_specs=[pl.BlockSpec(memory_space=VMEM)],
        out_specs=pl.BlockSpec(memory_space=VMEM),
    )(packed)


def project_kernel(fib_ref, basis_ref, core_ref, mine_ref, sent_ref, send_sem, recv_sem):
    gx = lax.axis_index("gx")
    z, core = gx // 2, gx % 2
    ycount = fib_ref.shape[0]
    per = ycount // GROUPS
    ranks = core_ref.shape[1]
    rows = mine_ref.shape[0]
    peers = []
    for dz in (4, 3, 5, 2, 6, 1, 7):
        for flip in (0, 1):
            peers.append(lax.rem(z + dz, 8) * 2 + (core if flip == 0 else 1 - core))
    peers.append(2 * z + (1 - core))
    barrier = pltpu.get_barrier_semaphore()
    for peer in peers:
        pl.semaphore_signal(barrier, inc=1, device_id={"gx": peer}, device_id_type=MESH)
    mine_ref[...] = basis_ref[pl.ds(pl.multiple_of(gx * rows, rows), rows), :]
    basis = split(basis_ref[...])
    for g in range(GROUPS):
        for y in range(per):
            sent_ref[g * per + y] = dot_split(basis, split(fib_ref[g * per + y]), 0, 0)
        if g == 0:
            pl.semaphore_wait(barrier, len(peers))
        here = pl.ds(g * per, per)
        there = pl.ds(gx * ycount + g * per, per)
        for peer in peers:
            pltpu.make_async_remote_copy(
                src_ref=sent_ref.at[here, pl.ds(pl.multiple_of(peer * ranks, ranks), ranks)],
                dst_ref=core_ref.at[there],
                send_sem=send_sem, recv_sem=recv_sem,
                device_id={"gx": peer}, device_id_type=MESH).start()
        pltpu.make_async_copy(
            sent_ref.at[here, pl.ds(pl.multiple_of(gx * ranks, ranks), ranks)],
            core_ref.at[there], recv_sem).start()
    pltpu.make_async_copy(core_ref, core_ref, recv_sem).wait()
    done = core_ref.at[pl.ds(0, 15 * ycount)]
    pltpu.make_async_copy(done, done, send_sem).wait()


def project(fib, basis):
    ycount = fib.shape[0]
    return pl.pallas_call(
        project_kernel,
        out_shape=(jax.ShapeDtypeStruct((GX * ycount, RANK // GX, BLOCK), jnp.float32),
                   jax.ShapeDtypeStruct((NX // GX, RANK), jnp.float32)),
        in_specs=[pl.BlockSpec(memory_space=VMEM)] * 2,
        out_specs=(pl.BlockSpec(memory_space=VMEM),) * 2,
        scratch_shapes=[VMEM((ycount, RANK, BLOCK), jnp.float32),
                        pltpu.SemaphoreType.DMA, pltpu.SemaphoreType.DMA],
        compiler_params=pltpu.CompilerParams(collective_id=1, has_side_effects=True),
    )(fib, basis)


def local(snapshot):
    fib, packed = gather_gram(jnp.transpose(snapshot, (1, 0, 2)))
    basis = make_basis(packed)
    returned, mine = project(fib, basis)
    return (mine, jnp.transpose(returned, (1, 0, 2)))


def solution(mesh):
    in_specs = (P("gx", "gy", "gz"),)
    out_specs = (P("gx", None), P("gx", "gy", "gz"))
    return jax.shard_map(local, mesh=mesh, in_specs=in_specs, out_specs=out_specs, check_vma=False)
```

```python
import jax
import jax.numpy as jnp
from jax import lax
from jax.experimental import pallas as pl
from jax.experimental.pallas import tpu as pltpu
from jax.sharding import PartitionSpec as P

RANK = 128
ITERS = 2
NX = 512
GX, GY, GZ = 16, 8, 4
MESH = pl.DeviceIdType.MESH
VMEM = pltpu.VMEM
BLOCK = 128
PLANE = GY * GZ
EARLY, LATE = 24, 8
FIRST = EARLY * GX
EARLY_PIECE, LATE_PIECE = 16, 8
SPLIT = 2
STEPS = 10


def split(x):
    hi = x.astype(jnp.bfloat16)
    lo = (x - hi.astype(jnp.float32)).astype(jnp.bfloat16)
    return hi, lo


def contract(a, b, ca, cb):
    return lax.dot_general(a, b, (((ca,), (cb,)), ((), ())), preferred_element_type=jnp.float32)


def dot_split(a, b, ca=1, cb=0):
    (ah, al), (bh, bl) = a, b
    return contract(ah, bh, ca, cb) + (contract(ah, bl, ca, cb) + contract(al, bh, ca, cb))


def column_peers():
    gx = lax.axis_index("gx")
    z, core = gx // 2, gx % 2
    peers = [2 * z + (1 - core)]
    for dz in (1, 7, 2, 6, 3, 5, 4):
        peers.append(lax.rem(z + dz, 8) * 2 + core)
        peers.append(lax.rem(z + dz, 8) * 2 + (1 - core))
    return peers


class Sum:
    def __init__(self, piece, acc, half, parts, levels, own, out, sems):
        self.piece, self.acc, self.half, self.parts = piece, acc, half, parts
        self.levels, self.own, self.out, self.sems = levels, own, out, sems
        self.rows = PLANE * piece
        gx, gy, gz = lax.axis_index("gx"), lax.axis_index("gy"), lax.axis_index("gz")
        self.z, self.core = gx // 2, gx % 2
        self.partner = {"gx": 2 * self.z + (1 - self.core)}
        self.slot = gy * GZ + gz
        self.mine = pl.multiple_of(self.core * self.rows, self.rows)
        self.other = pl.multiple_of((1 - self.core) * self.rows, self.rows)
        self.plane = []
        for dy in range(GY):
            for dx in range(GZ):
                if (dy, dx) != (0, 0):
                    ty, tx = lax.rem(gy + dy, GY), lax.rem(gz + dx, GZ)
                    self.plane.append((dy * GZ + dx - 1, ty * GZ + tx, {"gy": ty, "gz": tx}))
        self.at = pl.ds(pl.multiple_of(self.mine + self.slot * piece, 8), piece)

    def copy(self, src, dst, step, device):
        return pltpu.make_async_remote_copy(
            src_ref=src, dst_ref=dst, send_sem=self.sems.at[2 * step], recv_sem=self.sems.at[2 * step + 1],
            device_id=device, device_id_type=MESH)

    def taken(self, step, count):
        gone = self.acc.at[pl.ds(0, count * self.piece)]
        pltpu.make_async_copy(gone, gone, self.sems.at[2 * step]).wait()
        pltpu.make_async_copy(gone, gone, self.sems.at[2 * step + 1]).wait()

    def swap(self):
        return self.copy(self.acc.at[pl.ds(self.other, self.rows)], self.half, 0, self.partner)

    def back(self):
        return self.copy(self.out.at[pl.ds(self.mine, self.rows)], self.out.at[pl.ds(self.mine, self.rows)],
                         4, self.partner)

    def start_cores(self):
        self.swap().start()

    def start_plane(self):
        self.swap().wait()
        self.half[...] += self.acc[pl.ds(self.mine, self.rows), :]
        for n, theirs, device in self.plane:
            src = self.half.at[pl.ds(pl.multiple_of(theirs * self.piece, 8), self.piece)]
            self.copy(src, self.parts.at[n], 1, device).start()

    def start_levels(self):
        self.taken(1, PLANE - 1)
        total = self.half[pl.ds(pl.multiple_of(self.slot * self.piece, 8), self.piece), :]
        for n in range(PLANE - 1):
            total = total + self.parts[n]
        self.own[0] = total
        for dz in range(1, 8):
            device = {"gx": lax.rem(self.z + dz, 8) * 2 + self.core}
            self.copy(self.own.at[0], self.levels.at[dz - 1], 2, device).start()

    def start_gather(self):
        self.taken(2, 7)
        total = self.own[0]
        for n in range(7):
            total = total + self.levels[n]
        self.own[1] = total
        self.out[self.at, :] = total
        for n, theirs, device in self.plane:
            self.copy(self.own.at[1], self.out.at[self.at], 3, device).start()

    def start_back(self):
        self.taken(3, PLANE - 1)
        self.back().start()

    def finish(self):
        self.back().wait()


def gather_gram_kernel(snap_ref, fib_out, early_out, late_out, fib_ref,
                       acc_e, half_e, parts_e, levels_e, own_e,
                       acc_l, half_l, parts_l, levels_l, own_l,
                       send_sem, fib_sem, keep_sem, sems_e, sems_l):
    gx = lax.axis_index("gx")
    ycount = fib_ref.shape[0]
    per = ycount // SPLIT
    peers = column_peers()
    early = Sum(EARLY_PIECE, acc_e, half_e, parts_e, levels_e, own_e, early_out, sems_e)
    late = Sum(LATE_PIECE, acc_l, half_l, parts_l, levels_l, own_l, late_out, sems_l)

    barrier = pltpu.get_barrier_semaphore()
    for peer in peers:
        pl.semaphore_signal(barrier, inc=1, device_id={"gx": peer}, device_id_type=MESH)
    for n, theirs, device in early.plane:
        pl.semaphore_signal(barrier, inc=1, device_id=device, device_id_type=MESH)
    pl.semaphore_wait(barrier, len(peers) + len(early.plane))

    for part, (first, count, base) in enumerate(((0, EARLY, 0), (EARLY, LATE, FIRST))):
        place = pl.ds(pl.multiple_of(base + gx * count, 8), count)
        for g in range(SPLIT):
            sem = fib_sem.at[part * SPLIT + g]

            def send(step, carry):
                y = g * per + step
                pltpu.make_async_copy(
                    snap_ref.at[pl.ds(first, count), gx * ycount + y], fib_ref.at[y, place], sem).start()
                for peer in peers:
                    pltpu.make_async_remote_copy(
                        src_ref=snap_ref.at[pl.ds(first, count), peer * ycount + y],
                        dst_ref=fib_ref.at[y, place],
                        send_sem=send_sem, recv_sem=sem,
                        device_id={"gx": peer}, device_id_type=MESH).start()
                return carry

            lax.fori_loop(0, per, send, 0)

    acc_e[...] = jnp.zeros_like(acc_e)
    acc_l[...] = jnp.zeros_like(acc_l)

    def arrived(part, g, base, rows):
        here = fib_ref.at[pl.ds(g * per, per), pl.ds(base, rows)]
        pltpu.make_async_copy(here, here, fib_sem.at[part * SPLIT + g]).wait()
        pltpu.make_async_copy(here, fib_out.at[pl.ds(g * per, per), pl.ds(base, rows)], keep_sem).start()

    def add_early(y, carry):
        hi, lo = split(fib_ref[y, pl.ds(0, FIRST), :])
        at = 0
        for j in range(FIRST // BLOCK):
            b = j * BLOCK
            rows = FIRST - b
            acc_e[pl.ds(at, rows), :] += dot_split(
                (hi[b:], lo[b:]), (hi[b:b + BLOCK], lo[b:b + BLOCK]), 1, 1)
            at += rows
        return carry

    def add_late(y, carry):
        hi, lo = split(fib_ref[y])
        acc_l[...] += dot_split((hi, lo), (hi[FIRST:], lo[FIRST:]), 1, 1)
        return carry

    for g in range(SPLIT):
        arrived(0, g, 0, FIRST)
        lax.fori_loop(g * per, g * per + per, add_early, 0)
    early.start_cores()
    early.start_plane()
    early.start_levels()
    for g in range(SPLIT):
        arrived(1, g, FIRST, NX - FIRST)
        lax.fori_loop(g * per, g * per + per, add_late, 0)
    late.start_cores()
    late.start_plane()
    early.start_gather()
    late.start_levels()
    early.start_back()
    late.start_gather()
    early.finish()
    late.start_back()
    sent = fib_ref.at[:, pl.ds(0, NX - NX // GX)]
    pltpu.make_async_copy(sent, sent, send_sem).wait()
    pltpu.make_async_copy(fib_ref, fib_out, keep_sem).wait()
    late.finish()


def gather_gram(snap):
    ycount = snap.shape[1] // GX
    dma = pltpu.SemaphoreType.DMA

    def scratch(piece):
        rows = PLANE * piece
        return [VMEM((2 * rows, BLOCK), jnp.float32), VMEM((rows, BLOCK), jnp.float32),
                VMEM((PLANE - 1, piece, BLOCK), jnp.float32), VMEM((7, piece, BLOCK), jnp.float32),
                VMEM((2, piece, BLOCK), jnp.float32)]

    return pl.pallas_call(
        gather_gram_kernel,
        out_shape=(jax.ShapeDtypeStruct((ycount, NX, BLOCK), jnp.float32),
                   jax.ShapeDtypeStruct((2 * PLANE * EARLY_PIECE, BLOCK), jnp.float32),
                   jax.ShapeDtypeStruct((2 * PLANE * LATE_PIECE, BLOCK), jnp.float32)),
        in_specs=[pl.BlockSpec(memory_space=pl.ANY)],
        out_specs=(pl.BlockSpec(memory_space=pl.ANY), pl.BlockSpec(memory_space=VMEM),
                   pl.BlockSpec(memory_space=VMEM)),
        scratch_shapes=[VMEM((ycount, NX, BLOCK), jnp.float32)] + scratch(EARLY_PIECE) + scratch(LATE_PIECE)
        + [dma, dma((2 * SPLIT,)), dma, dma((STEPS,)), dma((STEPS,))],
        compiler_params=pltpu.CompilerParams(collective_id=0, has_side_effects=True),
    )(snap)


def inverse_factor(a):
    n = a.shape[0]
    tiles = [a[8 * t:8 * t + 8, :] for t in range(n // 8)]
    lane = lax.broadcasted_iota(jnp.int32, (8, n), 1)
    sub = lax.broadcasted_iota(jnp.int32, (8, n), 0)
    out = []
    for p in range(n // 8):
        base = 8 * p
        own = tiles[p]
        cols = [jnp.broadcast_to(own[:, base + j:base + j + 1], (8, n)) for j in range(8)]
        s = [[jnp.broadcast_to(cols[j][i:i + 1, :], (8, n)) for j in range(i + 1)] for i in range(8)]
        panel = (lane >= base) & (lane < base + 8)
        rows = [jnp.broadcast_to(own[j:j + 1, :], (8, n)) for j in range(8)]
        rows = [jnp.where(lane == base + j, 1.0, jnp.where(panel, 0.0, rows[j])) for j in range(8)]
        rinv, low = [], [[None] * 8 for _ in range(8)]
        for j in range(8):
            r = 1.0 / s[j][j]
            rinv.append(r)
            for i in range(j + 1, 8):
                low[i][j] = s[i][j] * r
            for i in range(j + 1, 8):
                for k in range(j + 1, i + 1):
                    s[i][k] = s[i][k] - low[i][j] * s[k][j]
        for j in range(8):
            for i in range(j):
                rows[j] = rows[j] - low[j][i] * rows[i]
        scaled = rows[0] * jnp.sqrt(rinv[0])
        for j in range(1, 8):
            scaled = jnp.where(sub == j, rows[j] * jnp.sqrt(rinv[j]), scaled)
        out.append(jnp.where(lane <= sub + base, scaled, 0.0))
        for t in range(p + 1, n // 8):
            tile = tiles[t]
            c = [jnp.broadcast_to(tile[:, base + j:base + j + 1], (8, n)) for j in range(8)]
            acc = jnp.where(panel, 0.0, tile)
            for j in range(8):
                for i in range(j):
                    c[j] = c[j] - c[i] * low[j][i]
            for j in range(8):
                acc = acc - (c[j] * rinv[j]) * rows[j]
            tiles[t] = acc
    return jnp.concatenate(out, axis=0)


def basis_project_kernel(early_ref, late_ref, fib_hbm, core_ref, mine_ref, fib_ref, hi_ref, lo_ref,
                         m_ref, bt_ref, b_ref, sent_ref, fib_sem, send_sem, recv_sem):
    gx = lax.axis_index("gx")
    ycount = fib_ref.shape[0]
    ranks = core_ref.shape[1]
    peers = column_peers()
    barrier = pltpu.get_barrier_semaphore()
    for peer in peers:
        pl.semaphore_signal(barrier, inc=1, device_id={"gx": peer}, device_id_type=MESH)
    load = pltpu.make_async_copy(fib_hbm, fib_ref, fib_sem)
    load.start()

    nb = NX // BLOCK
    blocks, at = {}, 0
    for j in range(nb - 1):
        for i in range(j, nb - 1):
            blocks[i, j] = early_ref[pl.ds(at, BLOCK), :]
            at += BLOCK
    for i in range(nb):
        blocks[i, nb - 1] = late_ref[pl.ds(i * BLOCK, BLOCK), :]
    for i in range(nb):
        for j in range(nb):
            if (i, j) not in blocks:
                blocks[i, j] = blocks[j, i].T
    rows = [jnp.concatenate([blocks[i, j] for j in range(nb)], axis=1) for i in range(nb)]
    for i in range(nb):
        hi, lo = split(rows[i])
        hi_ref[pl.ds(i * BLOCK, BLOCK), :] = hi
        lo_ref[pl.ds(i * BLOCK, BLOCK), :] = lo
    per_block = RANK // (EARLY + LATE)
    for n in range(per_block):
        m_ref[pl.ds(n * (EARLY + LATE), EARLY), :] = rows[0][n * EARLY:(n + 1) * EARLY]
        m_ref[pl.ds(n * (EARLY + LATE) + EARLY, LATE), :] = rows[nb - 1][n * LATE:(n + 1) * LATE]

    def iterate(step, carry):
        m = split(m_ref[...])
        basis = dot_split(split(inverse_factor(dot_split(m, m, 1, 1))), m)
        bt_ref[...] = basis

        @pl.when(step < ITERS)
        def _():
            m_ref[...] = dot_split(split(basis), (hi_ref[...], lo_ref[...]))

        return carry

    lax.fori_loop(0, ITERS + 1, iterate, 0)
    basis = split(bt_ref[...])
    load.wait()
    pl.semaphore_wait(barrier, len(peers))

    def emit(y, carry):
        sent_ref[y] = dot_split(basis, split(fib_ref[y]))
        there = core_ref.at[gx * ycount + y]
        for peer in peers:
            pltpu.make_async_remote_copy(
                src_ref=sent_ref.at[y, pl.ds(pl.multiple_of(peer * ranks, ranks), ranks)],
                dst_ref=there, send_sem=send_sem, recv_sem=recv_sem,
                device_id={"gx": peer}, device_id_type=MESH).start()
        pltpu.make_async_copy(
            sent_ref.at[y, pl.ds(pl.multiple_of(gx * ranks, ranks), ranks)], there, recv_sem).start()
        return carry

    lax.fori_loop(0, ycount, emit, 0)
    b_ref[...] = bt_ref[...].T
    mine_ref[pl.ds(0, EARLY), :] = b_ref[pl.ds(pl.multiple_of(gx * EARLY, 8), EARLY), :]
    mine_ref[pl.ds(EARLY, LATE), :] = b_ref[pl.ds(pl.multiple_of(FIRST + gx * LATE, 8), LATE), :]
    done = sent_ref.at[:, pl.ds(0, RANK - RANK // GX)]
    pltpu.make_async_copy(done, done, send_sem).wait()
    pltpu.make_async_copy(core_ref, core_ref, recv_sem).wait()


def basis_project(fib, early, late):
    ycount = fib.shape[0]
    dma = pltpu.SemaphoreType.DMA
    return pl.pallas_call(
        basis_project_kernel,
        out_shape=(jax.ShapeDtypeStruct((GX * ycount, RANK // GX, BLOCK), jnp.float32),
                   jax.ShapeDtypeStruct((NX // GX, RANK), jnp.float32)),
        in_specs=[pl.BlockSpec(memory_space=VMEM)] * 2 + [pl.BlockSpec(memory_space=pl.ANY)],
        out_specs=(pl.BlockSpec(memory_space=VMEM),) * 2,
        scratch_shapes=[VMEM((ycount, NX, BLOCK), jnp.float32),
                        VMEM((NX, NX), jnp.bfloat16), VMEM((NX, NX), jnp.bfloat16),
                        VMEM((RANK, NX), jnp.float32), VMEM((RANK, NX), jnp.float32),
                        VMEM((NX, RANK), jnp.float32), VMEM((ycount, RANK, BLOCK), jnp.float32),
                        dma, dma, dma],
        compiler_params=pltpu.CompilerParams(collective_id=1, has_side_effects=True),
    )(early, late, fib)


def local(snapshot):
    fib, early, late = gather_gram(snapshot)
    returned, mine = basis_project(fib, early, late)
    return (mine, jnp.transpose(returned, (1, 0, 2)))


def solution(mesh):
    in_specs = (P("gx", "gy", "gz"),)
    out_specs = (P("gx", None), P("gx", "gy", "gz"))
    return jax.shard_map(local, mesh=mesh, in_specs=in_specs, out_specs=out_specs, check_vma=False)
```

```python
import jax
import jax.numpy as jnp
from jax import lax
from jax.experimental import pallas as pl
from jax.experimental.pallas import tpu as pltpu
from jax.sharding import PartitionSpec as P

RANK = 128
ITERS = 2
NX = 512
GX, GY, GZ = 16, 8, 4
MESH = pl.DeviceIdType.MESH
VMEM = pltpu.VMEM
BLOCK = 128
PLANE = GY * GZ
EARLY, LATE = 24, 8
FIRST = EARLY * GX
EARLY_PIECE, LATE_PIECE = 16, 8
SPLIT = 5
STEPS = 10


def split(x):
    hi = x.astype(jnp.bfloat16)
    lo = (x - hi.astype(jnp.float32)).astype(jnp.bfloat16)
    return hi, lo


def contract(a, b, ca, cb):
    return lax.dot_general(a, b, (((ca,), (cb,)), ((), ())), preferred_element_type=jnp.float32)


def dot_split(a, b, ca=1, cb=0):
    (ah, al), (bh, bl) = a, b
    return contract(ah, bh, ca, cb) + (contract(ah, bl, ca, cb) + contract(al, bh, ca, cb))


def column_peers():
    gx = lax.axis_index("gx")
    z, core = gx // 2, gx % 2
    peers = [2 * z + (1 - core)]
    for dz in (1, 7, 2, 6, 3, 5, 4):
        peers.append(lax.rem(z + dz, 8) * 2 + core)
        peers.append(lax.rem(z + dz, 8) * 2 + (1 - core))
    return peers


class Sum:
    def __init__(self, piece, acc, half, parts, levels, own, out, sems):
        self.piece, self.acc, self.half, self.parts = piece, acc, half, parts
        self.levels, self.own, self.out, self.sems = levels, own, out, sems
        self.rows = PLANE * piece
        gx, gy, gz = lax.axis_index("gx"), lax.axis_index("gy"), lax.axis_index("gz")
        self.z, self.core = gx // 2, gx % 2
        self.partner = {"gx": 2 * self.z + (1 - self.core)}
        self.slot = gy * GZ + gz
        self.mine = pl.multiple_of(self.core * self.rows, self.rows)
        self.other = pl.multiple_of((1 - self.core) * self.rows, self.rows)
        self.plane = []
        for dy in range(GY):
            for dx in range(GZ):
                if (dy, dx) != (0, 0):
                    ty, tx = lax.rem(gy + dy, GY), lax.rem(gz + dx, GZ)
                    self.plane.append((dy * GZ + dx - 1, ty * GZ + tx, {"gy": ty, "gz": tx}))
        self.at = pl.ds(pl.multiple_of(self.mine + self.slot * piece, 8), piece)

    def copy(self, src, dst, step, device):
        return pltpu.make_async_remote_copy(
            src_ref=src, dst_ref=dst, send_sem=self.sems.at[2 * step], recv_sem=self.sems.at[2 * step + 1],
            device_id=device, device_id_type=MESH)

    def taken(self, step, count):
        gone = self.acc.at[pl.ds(0, count * self.piece)]
        pltpu.make_async_copy(gone, gone, self.sems.at[2 * step]).wait()
        pltpu.make_async_copy(gone, gone, self.sems.at[2 * step + 1]).wait()

    def swap(self):
        return self.copy(self.acc.at[pl.ds(self.other, self.rows)], self.half, 0, self.partner)

    def back(self):
        return self.copy(self.out.at[pl.ds(self.mine, self.rows)], self.out.at[pl.ds(self.mine, self.rows)],
                         4, self.partner)

    def start_cores(self):
        self.swap().start()

    def start_plane(self):
        self.swap().wait()
        self.half[...] += self.acc[pl.ds(self.mine, self.rows), :]
        for n, theirs, device in self.plane:
            src = self.half.at[pl.ds(pl.multiple_of(theirs * self.piece, 8), self.piece)]
            self.copy(src, self.parts.at[n], 1, device).start()

    def start_levels(self):
        self.taken(1, PLANE - 1)
        total = self.half[pl.ds(pl.multiple_of(self.slot * self.piece, 8), self.piece), :]
        for n in range(PLANE - 1):
            total = total + self.parts[n]
        self.own[0] = total
        for dz in range(1, 8):
            device = {"gx": lax.rem(self.z + dz, 8) * 2 + self.core}
            self.copy(self.own.at[0], self.levels.at[dz - 1], 2, device).start()

    def start_gather(self):
        self.taken(2, 7)
        total = self.own[0]
        for n in range(7):
            total = total + self.levels[n]
        self.own[1] = total
        self.out[self.at, :] = total
        for n, theirs, device in self.plane:
            self.copy(self.own.at[1], self.out.at[self.at], 3, device).start()

    def start_back(self):
        self.taken(3, PLANE - 1)
        self.back().start()

    def finish(self):
        self.back().wait()


def gather_gram_kernel(snap_ref, fib_out, early_out, late_out, fib_ref,
                       acc_e, half_e, parts_e, levels_e, own_e,
                       acc_l, half_l, parts_l, levels_l, own_l,
                       send_sem, fib_sem, keep_sem, sems_e, sems_l):
    gx = lax.axis_index("gx")
    ycount = fib_ref.shape[0]
    per = ycount // SPLIT
    peers = column_peers()
    early = Sum(EARLY_PIECE, acc_e, half_e, parts_e, levels_e, own_e, early_out, sems_e)
    late = Sum(LATE_PIECE, acc_l, half_l, parts_l, levels_l, own_l, late_out, sems_l)

    barrier = pltpu.get_barrier_semaphore()
    for peer in peers:
        pl.semaphore_signal(barrier, inc=1, device_id={"gx": peer}, device_id_type=MESH)
    for n, theirs, device in early.plane:
        pl.semaphore_signal(barrier, inc=1, device_id=device, device_id_type=MESH)
    pl.semaphore_wait(barrier, len(peers) + len(early.plane))

    place = pl.ds(pl.multiple_of(gx * EARLY, 8), EARLY)
    late_place = pl.ds(pl.multiple_of(FIRST + gx * LATE, 8), LATE)

    def keep(y, carry):
        column = gx * ycount + y
        pltpu.make_async_copy(
            snap_ref.at[pl.ds(0, EARLY), column], fib_ref.at[y, place], fib_sem.at[0]).start()
        pltpu.make_async_copy(
            snap_ref.at[pl.ds(EARLY, LATE), column], fib_ref.at[y, late_place], fib_sem.at[1 + y // per]).start()
        return carry

    for peer in peers:

        def send(y, carry):
            pltpu.make_async_remote_copy(
                src_ref=snap_ref.at[pl.ds(0, EARLY), peer * ycount + y],
                dst_ref=fib_ref.at[y, place],
                send_sem=send_sem, recv_sem=fib_sem.at[0],
                device_id={"gx": peer}, device_id_type=MESH).start()
            return carry

        lax.fori_loop(0, ycount, send, 0)

    def send_late(g, carry):
        for peer in peers:
            for step in range(per):
                y = g * per + step
                pltpu.make_async_remote_copy(
                    src_ref=snap_ref.at[pl.ds(EARLY, LATE), peer * ycount + y],
                    dst_ref=fib_ref.at[y, late_place],
                    send_sem=send_sem, recv_sem=fib_sem.at[1 + g],
                    device_id={"gx": peer}, device_id_type=MESH).start()
        return carry

    lax.fori_loop(0, SPLIT, send_late, 0)
    lax.fori_loop(0, ycount, keep, 0)

    acc_e[...] = jnp.zeros_like(acc_e)
    acc_l[...] = jnp.zeros_like(acc_l)

    def arrived(sem, first, count, base, rows):
        ys, xs = pl.ds(first, count), pl.ds(base, rows)
        here = fib_ref.at[ys, xs]
        pltpu.make_async_copy(here, here, fib_sem.at[sem]).wait()
        pltpu.make_async_copy(here, fib_out.at[ys, xs], keep_sem).start()

    def add_early(y, carry):
        hi, lo = split(fib_ref[y, pl.ds(0, FIRST), :])
        at = 0
        for j in range(FIRST // BLOCK):
            b = j * BLOCK
            rows = FIRST - b
            acc_e[pl.ds(at, rows), :] += dot_split(
                (hi[b:], lo[b:]), (hi[b:b + BLOCK], lo[b:b + BLOCK]), 1, 1)
            at += rows
        return carry

    def add_late(y, carry):
        hi, lo = split(fib_ref[y])
        acc_l[...] += dot_split((hi, lo), (hi[FIRST:], lo[FIRST:]), 1, 1)
        return carry

    arrived(0, 0, ycount, 0, FIRST)
    lax.fori_loop(0, ycount, add_early, 0)
    early.start_cores()
    early.start_plane()
    early.start_levels()

    def take_late(g, carry):
        arrived(1 + g, g * per, per, FIRST, NX - FIRST)
        return lax.fori_loop(g * per, g * per + per, add_late, carry)

    lax.fori_loop(0, SPLIT, take_late, 0)
    late.start_cores()
    late.start_plane()
    late.start_levels()
    early.start_gather()
    late.start_gather()
    early.start_back()
    late.start_back()
    early.finish()
    sent = fib_ref.at[:, pl.ds(0, NX - NX // GX)]
    pltpu.make_async_copy(sent, sent, send_sem).wait()
    pltpu.make_async_copy(fib_ref, fib_out, keep_sem).wait()
    late.finish()


def gather_gram(snap):
    ycount = snap.shape[1] // GX
    dma = pltpu.SemaphoreType.DMA

    def scratch(piece):
        rows = PLANE * piece
        return [VMEM((2 * rows, BLOCK), jnp.float32), VMEM((rows, BLOCK), jnp.float32),
                VMEM((PLANE - 1, piece, BLOCK), jnp.float32), VMEM((7, piece, BLOCK), jnp.float32),
                VMEM((2, piece, BLOCK), jnp.float32)]

    return pl.pallas_call(
        gather_gram_kernel,
        out_shape=(jax.ShapeDtypeStruct((ycount, NX, BLOCK), jnp.float32),
                   jax.ShapeDtypeStruct((2 * PLANE * EARLY_PIECE, BLOCK), jnp.float32),
                   jax.ShapeDtypeStruct((2 * PLANE * LATE_PIECE, BLOCK), jnp.float32)),
        in_specs=[pl.BlockSpec(memory_space=pl.ANY)],
        out_specs=(pl.BlockSpec(memory_space=pl.ANY), pl.BlockSpec(memory_space=VMEM),
                   pl.BlockSpec(memory_space=VMEM)),
        scratch_shapes=[VMEM((ycount, NX, BLOCK), jnp.float32)] + scratch(EARLY_PIECE) + scratch(LATE_PIECE)
        + [dma, dma((1 + SPLIT,)), dma, dma((STEPS,)), dma((STEPS,))],
        compiler_params=pltpu.CompilerParams(collective_id=0, has_side_effects=True),
    )(snap)


def inverse_factor(a):
    n = a.shape[0]
    count = n // 8
    tiles = [a[8 * t:8 * t + 8, :] for t in range(count)]
    lane = lax.broadcasted_iota(jnp.int32, (8, n), 1)
    sub = lax.broadcasted_iota(jnp.int32, (8, n), 0)
    spread = lane - sub
    out = []
    for p in range(count):
        base = 8 * p
        own = tiles[p]
        cols = [jnp.take_along_axis(own, jnp.full((8, n), base + j, jnp.int32), axis=1) for j in range(8)]
        s = [[jnp.broadcast_to(cols[j][i:i + 1, :], (8, n)) for j in range(i + 1)] for i in range(8)]
        panel = (lane >= base) & (lane < base + 8)
        ready = jnp.where(panel, jnp.where(spread == base, 1.0, 0.0), own)
        rows = [jnp.broadcast_to(ready[j:j + 1, :], (8, n)) for j in range(8)]
        rinv, low = [], [[None] * 8 for _ in range(8)]
        for j in range(8):
            r = 1.0 / s[j][j]
            rinv.append(r)
            for i in range(j + 1, 8):
                low[i][j] = s[i][j] * r
                for k in range(j + 1, i + 1):
                    s[i][k] = s[i][k] - low[i][j] * s[k][j]
                rows[i] = rows[i] - low[i][j] * rows[j]
        merged, pivots = rows[0], s[0][0]
        for j in range(1, 8):
            merged = jnp.where(sub == j, rows[j], merged)
            pivots = jnp.where(sub == j, s[j][j], pivots)
        out.append(jnp.where(spread <= base, merged * lax.rsqrt(pivots), 0.0))
        if p + 1 == count:
            break
        solved = [rows[j] * rinv[j] for j in range(8)]
        for j in range(7, 0, -1):
            for i in range(j):
                solved[i] = solved[i] - low[j][i] * solved[j]
        rest = range(p + 1, count)
        acc = {t: jnp.where(panel, 0.0, tiles[t]) for t in rest}
        first = p + 1
        for j in range(8):
            acc[first] = acc[first] - jnp.broadcast_to(tiles[first][:, base + j:base + j + 1], (8, n)) * solved[j]
        for t in range(p + 2, count):
            for j in range(8):
                acc[t] = acc[t] - jnp.broadcast_to(tiles[t][:, base + j:base + j + 1], (8, n)) * solved[j]
        for t in rest:
            tiles[t] = acc[t]
    return jnp.concatenate(out, axis=0)


def basis_project_kernel(early_ref, late_ref, fib_hbm, core_ref, mine_ref, fib_ref, hi_ref, lo_ref,
                         m_ref, bt_ref, b_ref, sent_ref, fib_sem, send_sem, recv_sem):
    gx = lax.axis_index("gx")
    ycount = fib_ref.shape[0]
    ranks = core_ref.shape[1]
    peers = column_peers()
    barrier = pltpu.get_barrier_semaphore()
    for peer in peers:
        pl.semaphore_signal(barrier, inc=1, device_id={"gx": peer}, device_id_type=MESH)
    load = pltpu.make_async_copy(fib_hbm, fib_ref, fib_sem)
    load.start()

    nb = NX // BLOCK
    blocks, at = {}, 0
    for j in range(nb - 1):
        for i in range(j, nb - 1):
            blocks[i, j] = early_ref[pl.ds(at, BLOCK), :]
            at += BLOCK
    for i in range(nb):
        blocks[i, nb - 1] = late_ref[pl.ds(i * BLOCK, BLOCK), :]
    for i in range(nb):
        for j in range(nb):
            if (i, j) not in blocks:
                blocks[i, j] = blocks[j, i].T
    rows = [jnp.concatenate([blocks[i, j] for j in range(nb)], axis=1) for i in range(nb)]
    for i in range(nb):
        hi, lo = split(rows[i])
        hi_ref[pl.ds(i * BLOCK, BLOCK), :] = hi
        lo_ref[pl.ds(i * BLOCK, BLOCK), :] = lo
    per_block = RANK // (EARLY + LATE)
    for n in range(per_block):
        m_ref[pl.ds(n * (EARLY + LATE), EARLY), :] = rows[0][n * EARLY:(n + 1) * EARLY]
        m_ref[pl.ds(n * (EARLY + LATE) + EARLY, LATE), :] = rows[nb - 1][n * LATE:(n + 1) * LATE]

    def iterate(step, carry):
        m = split(m_ref[...])
        basis = dot_split(split(inverse_factor(dot_split(m, m, 1, 1))), m)
        bt_ref[...] = basis

        @pl.when(step < ITERS)
        def _():
            m_ref[...] = dot_split(split(basis), (hi_ref[...], lo_ref[...]))

        return carry

    lax.fori_loop(0, ITERS + 1, iterate, 0)
    basis = split(bt_ref[...])
    load.wait()
    pl.semaphore_wait(barrier, len(peers))

    def emit(y, carry):
        sent_ref[y] = dot_split(basis, split(fib_ref[y]))
        there = core_ref.at[gx * ycount + y]
        for peer in peers:
            pltpu.make_async_remote_copy(
                src_ref=sent_ref.at[y, pl.ds(pl.multiple_of(peer * ranks, ranks), ranks)],
                dst_ref=there, send_sem=send_sem, recv_sem=recv_sem,
                device_id={"gx": peer}, device_id_type=MESH).start()
        pltpu.make_async_copy(
            sent_ref.at[y, pl.ds(pl.multiple_of(gx * ranks, ranks), ranks)], there, recv_sem).start()
        return carry

    lax.fori_loop(0, ycount, emit, 0)
    b_ref[...] = bt_ref[...].T
    mine_ref[pl.ds(0, EARLY), :] = b_ref[pl.ds(pl.multiple_of(gx * EARLY, 8), EARLY), :]
    mine_ref[pl.ds(EARLY, LATE), :] = b_ref[pl.ds(pl.multiple_of(FIRST + gx * LATE, 8), LATE), :]
    done = sent_ref.at[:, pl.ds(0, RANK - RANK // GX)]
    pltpu.make_async_copy(done, done, send_sem).wait()
    pltpu.make_async_copy(core_ref, core_ref, recv_sem).wait()


def basis_project(fib, early, late):
    ycount = fib.shape[0]
    dma = pltpu.SemaphoreType.DMA
    return pl.pallas_call(
        basis_project_kernel,
        out_shape=(jax.ShapeDtypeStruct((GX * ycount, RANK // GX, BLOCK), jnp.float32),
                   jax.ShapeDtypeStruct((NX // GX, RANK), jnp.float32)),
        in_specs=[pl.BlockSpec(memory_space=VMEM)] * 2 + [pl.BlockSpec(memory_space=pl.ANY)],
        out_specs=(pl.BlockSpec(memory_space=VMEM),) * 2,
        scratch_shapes=[VMEM((ycount, NX, BLOCK), jnp.float32),
                        VMEM((NX, NX), jnp.bfloat16), VMEM((NX, NX), jnp.bfloat16),
                        VMEM((RANK, NX), jnp.float32), VMEM((RANK, NX), jnp.float32),
                        VMEM((NX, RANK), jnp.float32), VMEM((ycount, RANK, BLOCK), jnp.float32),
                        dma, dma, dma],
        compiler_params=pltpu.CompilerParams(collective_id=1, has_side_effects=True),
    )(early, late, fib)


def local(snapshot):
    fib, early, late = gather_gram(snapshot)
    returned, mine = basis_project(fib, early, late)
    return (mine, jnp.transpose(returned, (1, 0, 2)))


def solution(mesh):
    in_specs = (P("gx", "gy", "gz"),)
    out_specs = (P("gx", None), P("gx", "gy", "gz"))
    return jax.shard_map(local, mesh=mesh, in_specs=in_specs, out_specs=out_specs, check_vma=False)
```

```python
import jax
import jax.numpy as jnp
from jax import lax
from jax.experimental import pallas as pl
from jax.experimental.pallas import tpu as pltpu
from jax.sharding import PartitionSpec as P

RANK = 128
ITERS = 2
NX = 512
GX, GY, GZ = 16, 8, 4
MESH = pl.DeviceIdType.MESH
VMEM = pltpu.VMEM
BLOCK = 128
PLANE = GY * GZ
EARLY, LATE = 24, 8
FIRST = EARLY * GX
EARLY_PIECE, LATE_PIECE = 16, 8
SPLIT = 5
STEPS = 10


def split(x):
    hi = x.astype(jnp.bfloat16)
    lo = (x - hi.astype(jnp.float32)).astype(jnp.bfloat16)
    return hi, lo


def contract(a, b, ca, cb):
    return lax.dot_general(a, b, (((ca,), (cb,)), ((), ())), preferred_element_type=jnp.float32)


def dot_split(a, b, ca=1, cb=0):
    (ah, al), (bh, bl) = a, b
    return contract(ah, bh, ca, cb) + (contract(ah, bl, ca, cb) + contract(al, bh, ca, cb))


def column_peers():
    gx = lax.axis_index("gx")
    z, core = gx // 2, gx % 2
    peers = [2 * z + (1 - core)]
    for distance in (1, 2, 3):
        for side in (core, 1 - core):
            for dz in (distance, 8 - distance):
                peers.append(lax.rem(z + dz, 8) * 2 + side)
    for side in (core, 1 - core):
        peers.append(lax.rem(z + 4, 8) * 2 + side)
    return peers


class Sum:
    def __init__(self, piece, acc, half, parts, levels, own, out, sems):
        self.piece, self.acc, self.half, self.parts = piece, acc, half, parts
        self.levels, self.own, self.out, self.sems = levels, own, out, sems
        self.rows = PLANE * piece
        gx, gy, gz = lax.axis_index("gx"), lax.axis_index("gy"), lax.axis_index("gz")
        self.z, self.core = gx // 2, gx % 2
        self.partner = {"gx": 2 * self.z + (1 - self.core)}
        self.slot = gy * GZ + gz
        self.mine = pl.multiple_of(self.core * self.rows, self.rows)
        self.other = pl.multiple_of((1 - self.core) * self.rows, self.rows)
        self.plane = []
        for dy in range(GY):
            for dx in range(GZ):
                if (dy, dx) != (0, 0):
                    ty, tx = lax.rem(gy + dy, GY), lax.rem(gz + dx, GZ)
                    self.plane.append((dy * GZ + dx - 1, ty * GZ + tx, {"gy": ty, "gz": tx}))
        self.at = pl.ds(pl.multiple_of(self.mine + self.slot * piece, 8), piece)

    def copy(self, src, dst, step, device):
        return pltpu.make_async_remote_copy(
            src_ref=src, dst_ref=dst, send_sem=self.sems.at[2 * step], recv_sem=self.sems.at[2 * step + 1],
            device_id=device, device_id_type=MESH)

    def taken(self, step, count):
        gone = self.acc.at[pl.ds(0, count * self.piece)]
        pltpu.make_async_copy(gone, gone, self.sems.at[2 * step]).wait()
        pltpu.make_async_copy(gone, gone, self.sems.at[2 * step + 1]).wait()

    def swap(self):
        return self.copy(self.acc.at[pl.ds(self.other, self.rows)], self.half, 0, self.partner)

    def back(self):
        return self.copy(self.out.at[pl.ds(self.mine, self.rows)], self.out.at[pl.ds(self.mine, self.rows)],
                         4, self.partner)

    def start_cores(self):
        self.swap().start()

    def start_plane(self):
        self.swap().wait()
        self.half[...] += self.acc[pl.ds(self.mine, self.rows), :]
        for n, theirs, device in self.plane:
            src = self.half.at[pl.ds(pl.multiple_of(theirs * self.piece, 8), self.piece)]
            self.copy(src, self.parts.at[n], 1, device).start()

    def start_levels(self):
        self.taken(1, PLANE - 1)
        total = self.half[pl.ds(pl.multiple_of(self.slot * self.piece, 8), self.piece), :]
        for n in range(PLANE - 1):
            total = total + self.parts[n]
        self.own[0] = total
        for dz in range(1, 8):
            device = {"gx": lax.rem(self.z + dz, 8) * 2 + self.core}
            self.copy(self.own.at[0], self.levels.at[dz - 1], 2, device).start()

    def start_gather(self):
        self.taken(2, 7)
        total = self.own[0]
        for n in range(7):
            total = total + self.levels[n]
        self.own[1] = total
        self.out[self.at, :] = total
        for n, theirs, device in self.plane:
            self.copy(self.own.at[1], self.out.at[self.at], 3, device).start()

    def start_back(self):
        self.taken(3, PLANE - 1)
        self.back().start()

    def finish(self):
        self.back().wait()


def gather_gram_kernel(snap_ref, fib_out, early_out, late_out, fib_ref,
                       acc_e, half_e, parts_e, levels_e, own_e,
                       acc_l, half_l, parts_l, levels_l, own_l,
                       send_sem, fib_sem, keep_sem, sems_e, sems_l):
    gx = lax.axis_index("gx")
    ycount = fib_ref.shape[0]
    per = ycount // SPLIT
    peers = column_peers()
    early = Sum(EARLY_PIECE, acc_e, half_e, parts_e, levels_e, own_e, early_out, sems_e)
    late = Sum(LATE_PIECE, acc_l, half_l, parts_l, levels_l, own_l, late_out, sems_l)

    barrier = pltpu.get_barrier_semaphore()
    for peer in peers:
        pl.semaphore_signal(barrier, inc=1, device_id={"gx": peer}, device_id_type=MESH)
    for n, theirs, device in early.plane:
        pl.semaphore_signal(barrier, inc=1, device_id=device, device_id_type=MESH)
    pl.semaphore_wait(barrier, len(peers) + len(early.plane))

    for part, (first, count, base) in enumerate(((0, EARLY, 0), (EARLY, LATE, FIRST))):
        place = pl.ds(pl.multiple_of(base + gx * count, 8), count)

        def send(y, carry):
            sem = fib_sem.at[part * SPLIT + y // per]
            pltpu.make_async_copy(
                snap_ref.at[pl.ds(first, count), gx * ycount + y], fib_ref.at[y, place], sem).start()
            for peer in peers:
                pltpu.make_async_remote_copy(
                    src_ref=snap_ref.at[pl.ds(first, count), peer * ycount + y],
                    dst_ref=fib_ref.at[y, place],
                    send_sem=send_sem, recv_sem=sem,
                    device_id={"gx": peer}, device_id_type=MESH).start()
            return carry

        lax.fori_loop(0, ycount, send, 0)

    acc_e[...] = jnp.zeros_like(acc_e)
    acc_l[...] = jnp.zeros_like(acc_l)

    def arrived(part, g, base, rows):
        ys, xs = pl.ds(g * per, per), pl.ds(base, rows)
        here = fib_ref.at[ys, xs]
        pltpu.make_async_copy(here, here, fib_sem.at[part * SPLIT + g]).wait()
        pltpu.make_async_copy(here, fib_out.at[ys, xs], keep_sem).start()

    def add_early(y, carry):
        hi, lo = split(fib_ref[y, pl.ds(0, FIRST), :])
        at = 0
        for j in range(FIRST // BLOCK):
            b = j * BLOCK
            rows = FIRST - b
            acc_e[pl.ds(at, rows), :] += dot_split(
                (hi[b:], lo[b:]), (hi[b:b + BLOCK], lo[b:b + BLOCK]), 1, 1)
            at += rows
        return carry

    def add_late(y, carry):
        hi, lo = split(fib_ref[y])
        acc_l[...] += dot_split((hi, lo), (hi[FIRST:], lo[FIRST:]), 1, 1)
        return carry

    def take_early(g, carry):
        arrived(0, g, 0, FIRST)
        return lax.fori_loop(g * per, g * per + per, add_early, carry)

    lax.fori_loop(0, SPLIT, take_early, 0)
    early.start_cores()
    early.start_plane()
    early.start_levels()

    def take_late(g, carry):
        arrived(1, g, FIRST, NX - FIRST)
        return lax.fori_loop(g * per, g * per + per, add_late, carry)

    lax.fori_loop(0, SPLIT, take_late, 0)
    late.start_cores()
    late.start_plane()
    late.start_levels()
    early.start_gather()
    late.start_gather()
    early.start_back()
    late.start_back()
    early.finish()
    sent = fib_ref.at[:, pl.ds(0, NX - NX // GX)]
    pltpu.make_async_copy(sent, sent, send_sem).wait()
    pltpu.make_async_copy(fib_ref, fib_out, keep_sem).wait()
    late.finish()


def gather_gram(snap):
    ycount = snap.shape[1] // GX
    dma = pltpu.SemaphoreType.DMA

    def scratch(piece):
        rows = PLANE * piece
        return [VMEM((2 * rows, BLOCK), jnp.float32), VMEM((rows, BLOCK), jnp.float32),
                VMEM((PLANE - 1, piece, BLOCK), jnp.float32), VMEM((7, piece, BLOCK), jnp.float32),
                VMEM((2, piece, BLOCK), jnp.float32)]

    return pl.pallas_call(
        gather_gram_kernel,
        out_shape=(jax.ShapeDtypeStruct((ycount, NX, BLOCK), jnp.float32),
                   jax.ShapeDtypeStruct((2 * PLANE * EARLY_PIECE, BLOCK), jnp.float32),
                   jax.ShapeDtypeStruct((2 * PLANE * LATE_PIECE, BLOCK), jnp.float32)),
        in_specs=[pl.BlockSpec(memory_space=pl.ANY)],
        out_specs=(pl.BlockSpec(memory_space=pl.ANY), pl.BlockSpec(memory_space=VMEM),
                   pl.BlockSpec(memory_space=VMEM)),
        scratch_shapes=[VMEM((ycount, NX, BLOCK), jnp.float32)] + scratch(EARLY_PIECE) + scratch(LATE_PIECE)
        + [dma, dma((2 * SPLIT,)), dma, dma((STEPS,)), dma((STEPS,))],
        compiler_params=pltpu.CompilerParams(collective_id=0, has_side_effects=True),
    )(snap)


def inverse_factor(a):
    n = a.shape[0]
    count = n // 8
    tiles = [a[8 * t:8 * t + 8, :] for t in range(count)]
    lane = lax.broadcasted_iota(jnp.int32, (8, n), 1)
    sub = lax.broadcasted_iota(jnp.int32, (8, n), 0)
    spread = lane - sub
    out = []
    for p in range(count):
        base = 8 * p
        own = tiles[p]
        cols = [jnp.take_along_axis(own, jnp.full((8, n), base + j, jnp.int32), axis=1) for j in range(8)]
        s = [[jnp.broadcast_to(cols[j][i:i + 1, :], (8, n)) for j in range(i + 1)] for i in range(8)]
        panel = (lane >= base) & (lane < base + 8)
        ready = jnp.where(panel, jnp.where(spread == base, 1.0, 0.0), own)
        rows = [jnp.broadcast_to(ready[j:j + 1, :], (8, n)) for j in range(8)]
        rinv, low = [], [[None] * 8 for _ in range(8)]
        for j in range(8):
            r = 1.0 / s[j][j]
            rinv.append(r)
            for i in range(j + 1, 8):
                low[i][j] = s[i][j] * r
                for k in range(j + 1, i + 1):
                    s[i][k] = s[i][k] - low[i][j] * s[k][j]
                rows[i] = rows[i] - low[i][j] * rows[j]
        merged, pivots = rows[0], s[0][0]
        for j in range(1, 8):
            merged = jnp.where(sub == j, rows[j], merged)
            pivots = jnp.where(sub == j, s[j][j], pivots)
        out.append(jnp.where(spread <= base, merged * lax.rsqrt(pivots), 0.0))
        if p + 1 == count:
            break
        solved = [rows[j] * rinv[j] for j in range(8)]
        for j in range(7, 0, -1):
            for i in range(j):
                solved[i] = solved[i] - low[j][i] * solved[j]
        rest = range(p + 1, count)
        acc = {t: jnp.where(panel, 0.0, tiles[t]) for t in rest}
        first = p + 1
        for j in range(8):
            acc[first] = acc[first] - jnp.broadcast_to(tiles[first][:, base + j:base + j + 1], (8, n)) * solved[j]
        for t in range(p + 2, count):
            for j in range(8):
                acc[t] = acc[t] - jnp.broadcast_to(tiles[t][:, base + j:base + j + 1], (8, n)) * solved[j]
        for t in rest:
            tiles[t] = acc[t]
    return jnp.concatenate(out, axis=0)


def basis_project_kernel(early_ref, late_ref, fib_hbm, core_ref, mine_ref, fib_ref, hi_ref, lo_ref,
                         m_ref, bt_ref, b_ref, sent_ref, fib_sem, send_sem, recv_sem):
    gx = lax.axis_index("gx")
    ycount = fib_ref.shape[0]
    ranks = core_ref.shape[0]
    peers = column_peers()
    barrier = pltpu.get_barrier_semaphore()
    for peer in peers:
        pl.semaphore_signal(barrier, inc=1, device_id={"gx": peer}, device_id_type=MESH)
    load = pltpu.make_async_copy(fib_hbm, fib_ref, fib_sem)
    load.start()

    nb = NX // BLOCK
    blocks, at = {}, 0
    for j in range(nb - 1):
        for i in range(j, nb - 1):
            blocks[i, j] = early_ref[pl.ds(at, BLOCK), :]
            at += BLOCK
    for i in range(nb):
        blocks[i, nb - 1] = late_ref[pl.ds(i * BLOCK, BLOCK), :]
    for i in range(nb):
        for j in range(nb):
            if (i, j) not in blocks:
                blocks[i, j] = blocks[j, i].T
    rows = [jnp.concatenate([blocks[i, j] for j in range(nb)], axis=1) for i in range(nb)]
    for i in range(nb):
        hi, lo = split(rows[i])
        hi_ref[pl.ds(i * BLOCK, BLOCK), :] = hi
        lo_ref[pl.ds(i * BLOCK, BLOCK), :] = lo
    per_block = RANK // (EARLY + LATE)
    for n in range(per_block):
        m_ref[pl.ds(n * (EARLY + LATE), EARLY), :] = rows[0][n * EARLY:(n + 1) * EARLY]
        m_ref[pl.ds(n * (EARLY + LATE) + EARLY, LATE), :] = rows[nb - 1][n * LATE:(n + 1) * LATE]

    def iterate(step, carry):
        m = split(m_ref[...])
        basis = dot_split(split(inverse_factor(dot_split(m, m, 1, 1))), m)
        bt_ref[...] = basis

        @pl.when(step < ITERS)
        def _():
            m_ref[...] = dot_split(split(basis), (hi_ref[...], lo_ref[...]))

        return carry

    lax.fori_loop(0, ITERS + 1, iterate, 0)
    basis = split(bt_ref[...])
    load.wait()
    pl.semaphore_wait(barrier, len(peers))

    def emit(y, carry):
        sent_ref[y] = dot_split(basis, split(fib_ref[y]))
        there = core_ref.at[:, gx * ycount + y]
        for peer in peers:
            pltpu.make_async_remote_copy(
                src_ref=sent_ref.at[y, pl.ds(pl.multiple_of(peer * ranks, ranks), ranks)],
                dst_ref=there, send_sem=send_sem, recv_sem=recv_sem,
                device_id={"gx": peer}, device_id_type=MESH).start()
        pltpu.make_async_copy(
            sent_ref.at[y, pl.ds(pl.multiple_of(gx * ranks, ranks), ranks)], there, recv_sem).start()
        return carry

    lax.fori_loop(0, ycount, emit, 0)
    b_ref[...] = bt_ref[...].T
    mine_ref[pl.ds(0, EARLY), :] = b_ref[pl.ds(pl.multiple_of(gx * EARLY, 8), EARLY), :]
    mine_ref[pl.ds(EARLY, LATE), :] = b_ref[pl.ds(pl.multiple_of(FIRST + gx * LATE, 8), LATE), :]
    done = sent_ref.at[:, pl.ds(0, RANK - RANK // GX)]
    pltpu.make_async_copy(done, done, send_sem).wait()
    pltpu.make_async_copy(core_ref, core_ref, recv_sem).wait()


def basis_project(fib, early, late):
    ycount = fib.shape[0]
    dma = pltpu.SemaphoreType.DMA
    return pl.pallas_call(
        basis_project_kernel,
        out_shape=(jax.ShapeDtypeStruct((RANK // GX, GX * ycount, BLOCK), jnp.float32),
                   jax.ShapeDtypeStruct((NX // GX, RANK), jnp.float32)),
        in_specs=[pl.BlockSpec(memory_space=VMEM)] * 2 + [pl.BlockSpec(memory_space=pl.ANY)],
        out_specs=(pl.BlockSpec(memory_space=VMEM),) * 2,
        scratch_shapes=[VMEM((ycount, NX, BLOCK), jnp.float32),
                        VMEM((NX, NX), jnp.bfloat16), VMEM((NX, NX), jnp.bfloat16),
                        VMEM((RANK, NX), jnp.float32), VMEM((RANK, NX), jnp.float32),
                        VMEM((NX, RANK), jnp.float32), VMEM((ycount, RANK, BLOCK), jnp.float32),
                        dma, dma, dma],
        compiler_params=pltpu.CompilerParams(collective_id=1, has_side_effects=True),
    )(early, late, fib)


def local(snapshot):
    fib, early, late = gather_gram(snapshot)
    core, mine = basis_project(fib, early, late)
    return (mine, core)


def solution(mesh):
    in_specs = (P("gx", "gy", "gz"),)
    out_specs = (P("gx", None), P("gx", "gy", "gz"))
    return jax.shard_map(local, mesh=mesh, in_specs=in_specs, out_specs=out_specs, check_vma=False)
```

```python
import jax
import jax.numpy as jnp
from jax import lax
from jax.experimental import pallas as pl
from jax.experimental.pallas import tpu as pltpu
from jax.sharding import PartitionSpec as P

RANK = 128
ITERS = 2
NX = 512
GX, GY, GZ = 16, 8, 4
MESH = pl.DeviceIdType.MESH
VMEM = pltpu.VMEM
BLOCK = 128
PLANE = GY * GZ
EARLY, LATE = 24, 8
FIRST = EARLY * GX
EARLY_PIECE, LATE_PIECE = 16, 8
SPLIT = 5
STEPS = 12


def split(x):
    hi = x.astype(jnp.bfloat16)
    lo = (x - hi.astype(jnp.float32)).astype(jnp.bfloat16)
    return hi, lo


def contract(a, b, ca, cb):
    return lax.dot_general(a, b, (((ca,), (cb,)), ((), ())), preferred_element_type=jnp.float32)


def dot_split(a, b, ca=1, cb=0):
    (ah, al), (bh, bl) = a, b
    return contract(ah, bh, ca, cb) + (contract(ah, bl, ca, cb) + contract(al, bh, ca, cb))


def column_peers():
    gx = lax.axis_index("gx")
    z, core = gx // 2, gx % 2
    peers = [2 * z + (1 - core)]
    for distance in (1, 2, 3):
        for side in (core, 1 - core):
            for dz in (distance, 8 - distance):
                peers.append(lax.rem(z + dz, 8) * 2 + side)
    for side in (core, 1 - core):
        peers.append(lax.rem(z + 4, 8) * 2 + side)
    return peers


class Sum:
    def __init__(self, piece, acc, half, parts, levels, own, out, sems):
        self.piece, self.acc, self.half, self.parts = piece, acc, half, parts
        self.levels, self.own, self.out, self.sems = levels, own, out, sems
        self.rows = PLANE * piece
        gx, gy, gz = lax.axis_index("gx"), lax.axis_index("gy"), lax.axis_index("gz")
        self.z, self.core = gx // 2, gx % 2
        self.partner = {"gx": 2 * self.z + (1 - self.core)}
        self.slot = gy * GZ + gz
        self.mine = pl.multiple_of(self.core * self.rows, self.rows)
        self.other = pl.multiple_of((1 - self.core) * self.rows, self.rows)
        self.near, self.far = [], []
        for dy in range(GY):
            for dx in range(GZ):
                hops = min(dy, GY - dy) + min(dx, GZ - dx)
                if hops:
                    ty, tx = lax.rem(gy + dy, GY), lax.rem(gz + dx, GZ)
                    side = self.near if hops <= 2 else self.far
                    side.append((dy * GZ + dx - 1, ty * GZ + tx, {"gy": ty, "gz": tx}))
        self.plane = self.far + self.near
        self.at = pl.ds(pl.multiple_of(self.mine + self.slot * piece, 8), piece)

    def copy(self, src, dst, step, device):
        return pltpu.make_async_remote_copy(
            src_ref=src, dst_ref=dst, send_sem=self.sems.at[2 * step], recv_sem=self.sems.at[2 * step + 1],
            device_id=device, device_id_type=MESH)

    def taken(self, step, count):
        gone = self.acc.at[pl.ds(0, count * self.piece)]
        pltpu.make_async_copy(gone, gone, self.sems.at[2 * step]).wait()
        pltpu.make_async_copy(gone, gone, self.sems.at[2 * step + 1]).wait()

    def swap(self):
        return self.copy(self.acc.at[pl.ds(self.other, self.rows)], self.half, 0, self.partner)

    def back(self):
        return self.copy(self.out.at[pl.ds(self.mine, self.rows)], self.out.at[pl.ds(self.mine, self.rows)],
                         4, self.partner)

    def start_cores(self):
        self.swap().start()

    def start_plane(self):
        self.swap().wait()
        self.half[...] += self.acc[pl.ds(self.mine, self.rows), :]
        for step, side in ((5, self.far), (1, self.near)):
            for n, theirs, device in side:
                src = self.half.at[pl.ds(pl.multiple_of(theirs * self.piece, 8), self.piece)]
                self.copy(src, self.parts.at[n], step, device).start()

    def near_arrived(self):
        self.taken(1, len(self.near))

    def start_levels(self):
        self.taken(5, len(self.far))
        total = self.half[pl.ds(pl.multiple_of(self.slot * self.piece, 8), self.piece), :]
        for n in range(PLANE - 1):
            total = total + self.parts[n]
        self.own[0] = total
        for dz in range(1, 8):
            device = {"gx": lax.rem(self.z + dz, 8) * 2 + self.core}
            self.copy(self.own.at[0], self.levels.at[dz - 1], 2, device).start()

    def start_gather(self):
        self.taken(2, 7)
        total = self.own[0]
        for n in range(7):
            total = total + self.levels[n]
        self.own[1] = total
        self.out[self.at, :] = total
        for n, theirs, device in self.plane:
            self.copy(self.own.at[1], self.out.at[self.at], 3, device).start()

    def start_back(self):
        self.taken(3, PLANE - 1)
        self.back().start()

    def finish(self):
        self.back().wait()


def gather_gram_kernel(snap_ref, fib_out, early_out, late_out, fib_ref,
                       acc_e, half_e, parts_e, levels_e, own_e,
                       acc_l, half_l, parts_l, levels_l, own_l,
                       send_sem, fib_sem, keep_sem, sems_e, sems_l):
    gx = lax.axis_index("gx")
    ycount = fib_ref.shape[0]
    per = ycount // SPLIT
    peers = column_peers()
    early = Sum(EARLY_PIECE, acc_e, half_e, parts_e, levels_e, own_e, early_out, sems_e)
    late = Sum(LATE_PIECE, acc_l, half_l, parts_l, levels_l, own_l, late_out, sems_l)

    barrier = pltpu.get_barrier_semaphore()
    for peer in peers:
        pl.semaphore_signal(barrier, inc=1, device_id={"gx": peer}, device_id_type=MESH)
    for n, theirs, device in early.plane:
        pl.semaphore_signal(barrier, inc=1, device_id=device, device_id_type=MESH)
    pl.semaphore_wait(barrier, len(peers) + len(early.plane))

    for part, (first, count, base) in enumerate(((0, EARLY, 0), (EARLY, LATE, FIRST))):
        place = pl.ds(pl.multiple_of(base + gx * count, 8), count)

        def send(y, carry):
            sem = fib_sem.at[part * SPLIT + y // per]
            pltpu.make_async_copy(
                snap_ref.at[pl.ds(first, count), gx * ycount + y], fib_ref.at[y, place], sem).start()
            for peer in peers:
                pltpu.make_async_remote_copy(
                    src_ref=snap_ref.at[pl.ds(first, count), peer * ycount + y],
                    dst_ref=fib_ref.at[y, place],
                    send_sem=send_sem, recv_sem=sem,
                    device_id={"gx": peer}, device_id_type=MESH).start()
            return carry

        lax.fori_loop(0, ycount, send, 0)

    acc_e[...] = jnp.zeros_like(acc_e)
    acc_l[...] = jnp.zeros_like(acc_l)

    def arrived(part, g, base, rows):
        ys, xs = pl.ds(g * per, per), pl.ds(base, rows)
        here = fib_ref.at[ys, xs]
        pltpu.make_async_copy(here, here, fib_sem.at[part * SPLIT + g]).wait()
        pltpu.make_async_copy(here, fib_out.at[ys, xs], keep_sem).start()

    def add_early(y, carry):
        hi, lo = split(fib_ref[y, pl.ds(0, FIRST), :])
        at = 0
        for j in range(FIRST // BLOCK):
            b = j * BLOCK
            rows = FIRST - b
            acc_e[pl.ds(at, rows), :] += dot_split(
                (hi[b:], lo[b:]), (hi[b:b + BLOCK], lo[b:b + BLOCK]), 1, 1)
            at += rows
        return carry

    def add_late(y, carry):
        hi, lo = split(fib_ref[y])
        acc_l[...] += dot_split((hi, lo), (hi[FIRST:], lo[FIRST:]), 1, 1)
        return carry

    def take_early(g, carry):
        arrived(0, g, 0, FIRST)
        return lax.fori_loop(g * per, g * per + per, add_early, carry)

    lax.fori_loop(0, SPLIT, take_early, 0)
    early.start_cores()
    early.start_plane()
    early.near_arrived()
    early.start_levels()

    def take_late(g, carry):
        arrived(1, g, FIRST, NX - FIRST)
        return lax.fori_loop(g * per, g * per + per, add_late, carry)

    lax.fori_loop(0, SPLIT, take_late, 0)
    late.start_cores()
    late.start_plane()
    late.near_arrived()
    early.start_gather()
    late.start_levels()
    late.start_gather()
    early.start_back()
    late.start_back()
    early.finish()
    sent = fib_ref.at[:, pl.ds(0, NX - NX // GX)]
    pltpu.make_async_copy(sent, sent, send_sem).wait()
    pltpu.make_async_copy(fib_ref, fib_out, keep_sem).wait()
    late.finish()


def gather_gram(snap):
    ycount = snap.shape[1] // GX
    dma = pltpu.SemaphoreType.DMA

    def scratch(piece):
        rows = PLANE * piece
        return [VMEM((2 * rows, BLOCK), jnp.float32), VMEM((rows, BLOCK), jnp.float32),
                VMEM((PLANE - 1, piece, BLOCK), jnp.float32), VMEM((7, piece, BLOCK), jnp.float32),
                VMEM((2, piece, BLOCK), jnp.float32)]

    return pl.pallas_call(
        gather_gram_kernel,
        out_shape=(jax.ShapeDtypeStruct((ycount, NX, BLOCK), jnp.float32),
                   jax.ShapeDtypeStruct((2 * PLANE * EARLY_PIECE, BLOCK), jnp.float32),
                   jax.ShapeDtypeStruct((2 * PLANE * LATE_PIECE, BLOCK), jnp.float32)),
        in_specs=[pl.BlockSpec(memory_space=pl.ANY)],
        out_specs=(pl.BlockSpec(memory_space=pl.ANY), pl.BlockSpec(memory_space=VMEM),
                   pl.BlockSpec(memory_space=VMEM)),
        scratch_shapes=[VMEM((ycount, NX, BLOCK), jnp.float32)] + scratch(EARLY_PIECE) + scratch(LATE_PIECE)
        + [dma, dma((2 * SPLIT,)), dma, dma((STEPS,)), dma((STEPS,))],
        compiler_params=pltpu.CompilerParams(collective_id=0, has_side_effects=True),
    )(snap)


def inverse_factor(a):
    n = a.shape[0]
    count = n // 8
    tiles = [a[8 * t:8 * t + 8, :] for t in range(count)]
    lane = lax.broadcasted_iota(jnp.int32, (8, n), 1)
    sub = lax.broadcasted_iota(jnp.int32, (8, n), 0)
    spread = lane - sub
    out = []
    for p in range(count):
        base = 8 * p
        own = tiles[p]
        cols = [jnp.take_along_axis(own, jnp.full((8, n), base + j, jnp.int32), axis=1) for j in range(8)]
        s = [[jnp.broadcast_to(cols[j][i:i + 1, :], (8, n)) for j in range(i + 1)] for i in range(8)]
        panel = (lane >= base) & (lane < base + 8)
        ready = jnp.where(panel, jnp.where(spread == base, 1.0, 0.0), own)
        rows = [jnp.broadcast_to(ready[j:j + 1, :], (8, n)) for j in range(8)]
        rinv, low = [], [[None] * 8 for _ in range(8)]
        for j in range(8):
            r = 1.0 / s[j][j]
            rinv.append(r)
            for i in range(j + 1, 8):
                low[i][j] = s[i][j] * r
                for k in range(j + 1, i + 1):
                    s[i][k] = s[i][k] - low[i][j] * s[k][j]
                rows[i] = rows[i] - low[i][j] * rows[j]
        merged, pivots = rows[0], s[0][0]
        for j in range(1, 8):
            merged = jnp.where(sub == j, rows[j], merged)
            pivots = jnp.where(sub == j, s[j][j], pivots)
        out.append(jnp.where(spread <= base, merged * lax.rsqrt(pivots), 0.0))
        if p + 1 == count:
            break
        solved = [rows[j] * rinv[j] for j in range(8)]
        for j in range(7, 0, -1):
            for i in range(j):
                solved[i] = solved[i] - low[j][i] * solved[j]
        rest = range(p + 1, count)
        acc = {t: jnp.where(panel, 0.0, tiles[t]) for t in rest}
        first = p + 1
        for j in range(8):
            acc[first] = acc[first] - jnp.broadcast_to(tiles[first][:, base + j:base + j + 1], (8, n)) * solved[j]
        for t in range(p + 2, count):
            for j in range(8):
                acc[t] = acc[t] - jnp.broadcast_to(tiles[t][:, base + j:base + j + 1], (8, n)) * solved[j]
        for t in rest:
            tiles[t] = acc[t]
    return jnp.concatenate(out, axis=0)


def basis_project_kernel(early_ref, late_ref, fib_hbm, core_ref, mine_ref, fib_ref, hi_ref, lo_ref,
                         m_ref, bt_ref, b_ref, sent_ref, fib_sem, send_sem, recv_sem):
    gx = lax.axis_index("gx")
    ycount = fib_ref.shape[0]
    ranks = core_ref.shape[0]
    peers = column_peers()
    barrier = pltpu.get_barrier_semaphore()
    for peer in peers:
        pl.semaphore_signal(barrier, inc=1, device_id={"gx": peer}, device_id_type=MESH)
    load = pltpu.make_async_copy(fib_hbm, fib_ref, fib_sem)
    load.start()

    nb = NX // BLOCK
    blocks, at = {}, 0
    for j in range(nb - 1):
        for i in range(j, nb - 1):
            blocks[i, j] = early_ref[pl.ds(at, BLOCK), :]
            at += BLOCK
    for i in range(nb):
        blocks[i, nb - 1] = late_ref[pl.ds(i * BLOCK, BLOCK), :]
    for i in range(nb):
        for j in range(nb):
            if (i, j) not in blocks:
                blocks[i, j] = blocks[j, i].T
    rows = [jnp.concatenate([blocks[i, j] for j in range(nb)], axis=1) for i in range(nb)]
    for i in range(nb):
        hi, lo = split(rows[i])
        hi_ref[pl.ds(i * BLOCK, BLOCK), :] = hi
        lo_ref[pl.ds(i * BLOCK, BLOCK), :] = lo
    per_block = RANK // (EARLY + LATE)
    for n in range(per_block):
        m_ref[pl.ds(n * (EARLY + LATE), EARLY), :] = rows[0][n * EARLY:(n + 1) * EARLY]
        m_ref[pl.ds(n * (EARLY + LATE) + EARLY, LATE), :] = rows[nb - 1][n * LATE:(n + 1) * LATE]

    def iterate(step, carry):
        m = split(m_ref[...])
        basis = dot_split(split(inverse_factor(dot_split(m, m, 1, 1))), m)
        bt_ref[...] = basis

        @pl.when(step < ITERS)
        def _():
            m_ref[...] = dot_split(split(basis), (hi_ref[...], lo_ref[...]))

        return carry

    lax.fori_loop(0, ITERS + 1, iterate, 0)
    basis = split(bt_ref[...])
    load.wait()
    pl.semaphore_wait(barrier, len(peers))

    def emit(y, carry):
        sent_ref[y] = dot_split(basis, split(fib_ref[y]))
        there = core_ref.at[:, gx * ycount + y]
        for peer in peers:
            pltpu.make_async_remote_copy(
                src_ref=sent_ref.at[y, pl.ds(pl.multiple_of(peer * ranks, ranks), ranks)],
                dst_ref=there, send_sem=send_sem, recv_sem=recv_sem,
                device_id={"gx": peer}, device_id_type=MESH).start()
        pltpu.make_async_copy(
            sent_ref.at[y, pl.ds(pl.multiple_of(gx * ranks, ranks), ranks)], there, recv_sem).start()
        return carry

    lax.fori_loop(0, ycount, emit, 0)
    b_ref[...] = bt_ref[...].T
    mine_ref[pl.ds(0, EARLY), :] = b_ref[pl.ds(pl.multiple_of(gx * EARLY, 8), EARLY), :]
    mine_ref[pl.ds(EARLY, LATE), :] = b_ref[pl.ds(pl.multiple_of(FIRST + gx * LATE, 8), LATE), :]
    done = sent_ref.at[:, pl.ds(0, RANK - RANK // GX)]
    pltpu.make_async_copy(done, done, send_sem).wait()
    pltpu.make_async_copy(core_ref, core_ref, recv_sem).wait()


def basis_project(fib, early, late):
    ycount = fib.shape[0]
    dma = pltpu.SemaphoreType.DMA
    return pl.pallas_call(
        basis_project_kernel,
        out_shape=(jax.ShapeDtypeStruct((RANK // GX, GX * ycount, BLOCK), jnp.float32),
                   jax.ShapeDtypeStruct((NX // GX, RANK), jnp.float32)),
        in_specs=[pl.BlockSpec(memory_space=VMEM)] * 2 + [pl.BlockSpec(memory_space=pl.ANY)],
        out_specs=(pl.BlockSpec(memory_space=VMEM),) * 2,
        scratch_shapes=[VMEM((ycount, NX, BLOCK), jnp.float32),
                        VMEM((NX, NX), jnp.bfloat16), VMEM((NX, NX), jnp.bfloat16),
                        VMEM((RANK, NX), jnp.float32), VMEM((RANK, NX), jnp.float32),
                        VMEM((NX, RANK), jnp.float32), VMEM((ycount, RANK, BLOCK), jnp.float32),
                        dma, dma, dma],
        compiler_params=pltpu.CompilerParams(collective_id=1, has_side_effects=True),
    )(early, late, fib)


def finish_kernel(core_ref, mine_ref, core_out, mine_out):
    core_out[...] = core_ref[...]
    mine_out[...] = mine_ref[...]


def finish(core, mine):
    return pl.pallas_call(
        finish_kernel,
        out_shape=(jax.ShapeDtypeStruct(core.shape, core.dtype), jax.ShapeDtypeStruct(mine.shape, mine.dtype)),
        in_specs=[pl.BlockSpec(memory_space=VMEM)] * 2,
        out_specs=(pl.BlockSpec(memory_space=VMEM),) * 2,
    )(core, mine)


def local(snapshot):
    fib, early, late = gather_gram(snapshot)
    core, mine = basis_project(fib, early, late)
    core, mine = finish(core, mine)
    return (mine, core)


def solution(mesh):
    in_specs = (P("gx", "gy", "gz"),)
    out_specs = (P("gx", None), P("gx", "gy", "gz"))
    return jax.shard_map(local, mesh=mesh, in_specs=in_specs, out_specs=out_specs, check_vma=False)
```

```python
import jax
import jax.numpy as jnp
from jax import lax
from jax.experimental import pallas as pl
from jax.experimental.pallas import tpu as pltpu
from jax.sharding import PartitionSpec as P

RANK = 128
ITERS = 2
NX = 512
GX, GY, GZ = 16, 8, 4
MESH = pl.DeviceIdType.MESH
VMEM = pltpu.VMEM
BLOCK = 128
PLANE = GY * GZ
EARLY, LATE = 24, 8
FIRST = EARLY * GX
EARLY_PIECE, LATE_PIECE = 16, 8
SPLIT = 5
STEPS = 12


def split(x):
    hi = x.astype(jnp.bfloat16)
    lo = (x - hi.astype(jnp.float32)).astype(jnp.bfloat16)
    return hi, lo


def contract(a, b, ca, cb):
    return lax.dot_general(a, b, (((ca,), (cb,)), ((), ())), preferred_element_type=jnp.float32)


def dot_split(a, b, ca=1, cb=0):
    (ah, al), (bh, bl) = a, b
    return contract(ah, bh, ca, cb) + (contract(ah, bl, ca, cb) + contract(al, bh, ca, cb))


def column_peers():
    gx = lax.axis_index("gx")
    z, core = gx // 2, gx % 2
    peers = [2 * z + (1 - core)]
    for distance in (1, 2, 3):
        for side in (core, 1 - core):
            for dz in (distance, 8 - distance):
                peers.append(lax.rem(z + dz, 8) * 2 + side)
    for side in (core, 1 - core):
        peers.append(lax.rem(z + 4, 8) * 2 + side)
    return peers


class Sum:
    def __init__(self, piece, acc, half, parts, levels, own, out, sems):
        self.piece, self.acc, self.half, self.parts = piece, acc, half, parts
        self.levels, self.own, self.out, self.sems = levels, own, out, sems
        self.rows = PLANE * piece
        gx, gy, gz = lax.axis_index("gx"), lax.axis_index("gy"), lax.axis_index("gz")
        self.z, self.core = gx // 2, gx % 2
        self.partner = {"gx": 2 * self.z + (1 - self.core)}
        self.slot = gy * GZ + gz
        self.mine = pl.multiple_of(self.core * self.rows, self.rows)
        self.other = pl.multiple_of((1 - self.core) * self.rows, self.rows)
        self.near, self.far = [], []
        for dy in range(GY):
            for dx in range(GZ):
                hops = min(dy, GY - dy) + min(dx, GZ - dx)
                if hops:
                    ty, tx = lax.rem(gy + dy, GY), lax.rem(gz + dx, GZ)
                    side = self.near if hops <= 2 else self.far
                    side.append((dy * GZ + dx - 1, ty * GZ + tx, {"gy": ty, "gz": tx}))
        self.plane = self.far + self.near
        self.at = pl.ds(pl.multiple_of(self.mine + self.slot * piece, 8), piece)

    def copy(self, src, dst, step, device):
        return pltpu.make_async_remote_copy(
            src_ref=src, dst_ref=dst, send_sem=self.sems.at[2 * step], recv_sem=self.sems.at[2 * step + 1],
            device_id=device, device_id_type=MESH)

    def taken(self, step, count):
        gone = self.acc.at[pl.ds(0, count * self.piece)]
        pltpu.make_async_copy(gone, gone, self.sems.at[2 * step]).wait()
        pltpu.make_async_copy(gone, gone, self.sems.at[2 * step + 1]).wait()

    def swap(self):
        return self.copy(self.acc.at[pl.ds(self.other, self.rows)], self.half, 0, self.partner)

    def back(self):
        return self.copy(self.out.at[pl.ds(self.mine, self.rows)], self.out.at[pl.ds(self.mine, self.rows)],
                         4, self.partner)

    def start_cores(self):
        self.swap().start()

    def start_plane(self):
        self.swap().wait()
        self.half[...] += self.acc[pl.ds(self.mine, self.rows), :]
        for step, side in ((5, self.far), (1, self.near)):
            for n, theirs, device in side:
                src = self.half.at[pl.ds(pl.multiple_of(theirs * self.piece, 8), self.piece)]
                self.copy(src, self.parts.at[n], step, device).start()

    def near_arrived(self):
        self.taken(1, len(self.near))

    def start_levels(self):
        self.taken(5, len(self.far))
        total = self.half[pl.ds(pl.multiple_of(self.slot * self.piece, 8), self.piece), :]
        for n in range(PLANE - 1):
            total = total + self.parts[n]
        self.own[0] = total
        for dz in range(1, 8):
            device = {"gx": lax.rem(self.z + dz, 8) * 2 + self.core}
            self.copy(self.own.at[0], self.levels.at[dz - 1], 2, device).start()

    def start_gather(self):
        self.taken(2, 7)
        total = self.own[0]
        for n in range(7):
            total = total + self.levels[n]
        self.own[1] = total
        self.out[self.at, :] = total
        for n, theirs, device in self.plane:
            self.copy(self.own.at[1], self.out.at[self.at], 3, device).start()

    def start_back(self):
        self.taken(3, PLANE - 1)
        self.back().start()

    def finish(self):
        self.back().wait()


def gather_gram_kernel(snap_ref, fib_out, early_out, late_out, fib_ref,
                       acc_e, half_e, parts_e, levels_e, own_e,
                       acc_l, half_l, parts_l, levels_l, own_l,
                       send_sem, fib_sem, keep_sem, sems_e, sems_l):
    gx = lax.axis_index("gx")
    ycount = fib_ref.shape[0]
    per = ycount // SPLIT
    peers = column_peers()
    early = Sum(EARLY_PIECE, acc_e, half_e, parts_e, levels_e, own_e, early_out, sems_e)
    late = Sum(LATE_PIECE, acc_l, half_l, parts_l, levels_l, own_l, late_out, sems_l)

    barrier = pltpu.get_barrier_semaphore()
    for peer in peers:
        pl.semaphore_signal(barrier, inc=1, device_id={"gx": peer}, device_id_type=MESH)
    for n, theirs, device in early.plane:
        pl.semaphore_signal(barrier, inc=1, device_id=device, device_id_type=MESH)
    pl.semaphore_wait(barrier, len(peers) + len(early.plane))

    for part, (first, count, base) in enumerate(((0, EARLY, 0), (EARLY, LATE, FIRST))):
        place = pl.ds(pl.multiple_of(base + gx * count, 8), count)

        def send(y, carry):
            sem = fib_sem.at[part * SPLIT + y // per]
            pltpu.make_async_copy(
                snap_ref.at[pl.ds(first, count), gx * ycount + y], fib_ref.at[y, place], sem).start()
            for peer in peers:
                pltpu.make_async_remote_copy(
                    src_ref=snap_ref.at[pl.ds(first, count), peer * ycount + y],
                    dst_ref=fib_ref.at[y, place],
                    send_sem=send_sem, recv_sem=sem,
                    device_id={"gx": peer}, device_id_type=MESH).start()
            return carry

        lax.fori_loop(0, ycount, send, 0)

    acc_e[...] = jnp.zeros_like(acc_e)
    acc_l[...] = jnp.zeros_like(acc_l)

    def arrived(part, g, base, rows):
        ys, xs = pl.ds(g * per, per), pl.ds(base, rows)
        here = fib_ref.at[ys, xs]
        pltpu.make_async_copy(here, here, fib_sem.at[part * SPLIT + g]).wait()
        pltpu.make_async_copy(here, fib_out.at[ys, xs], keep_sem).start()

    def add_early(y, carry):
        hi, lo = split(fib_ref[y, pl.ds(0, FIRST), :])
        at = 0
        for j in range(FIRST // BLOCK):
            b = j * BLOCK
            rows = FIRST - b
            acc_e[pl.ds(at, rows), :] += dot_split(
                (hi[b:], lo[b:]), (hi[b:b + BLOCK], lo[b:b + BLOCK]), 1, 1)
            at += rows
        return carry

    def add_late(y, carry):
        hi, lo = split(fib_ref[y])
        acc_l[...] += dot_split((hi, lo), (hi[FIRST:], lo[FIRST:]), 1, 1)
        return carry

    def take_early(g, carry):
        arrived(0, g, 0, FIRST)
        return lax.fori_loop(g * per, g * per + per, add_early, carry)

    lax.fori_loop(0, SPLIT, take_early, 0)
    early.start_cores()
    early.start_plane()
    early.near_arrived()
    early.start_levels()

    def take_late(g, carry):
        arrived(1, g, FIRST, NX - FIRST)
        return lax.fori_loop(g * per, g * per + per, add_late, carry)

    lax.fori_loop(0, SPLIT, take_late, 0)
    late.start_cores()
    late.start_plane()
    late.near_arrived()
    early.start_gather()
    late.start_levels()
    late.start_gather()
    early.start_back()
    late.start_back()
    early.finish()
    sent = fib_ref.at[:, pl.ds(0, NX - NX // GX)]
    pltpu.make_async_copy(sent, sent, send_sem).wait()
    pltpu.make_async_copy(fib_ref, fib_out, keep_sem).wait()
    late.finish()


def gather_gram(snap):
    ycount = snap.shape[1] // GX
    dma = pltpu.SemaphoreType.DMA

    def scratch(piece):
        rows = PLANE * piece
        return [VMEM((2 * rows, BLOCK), jnp.float32), VMEM((rows, BLOCK), jnp.float32),
                VMEM((PLANE - 1, piece, BLOCK), jnp.float32), VMEM((7, piece, BLOCK), jnp.float32),
                VMEM((2, piece, BLOCK), jnp.float32)]

    return pl.pallas_call(
        gather_gram_kernel,
        out_shape=(jax.ShapeDtypeStruct((ycount, NX, BLOCK), jnp.float32),
                   jax.ShapeDtypeStruct((2 * PLANE * EARLY_PIECE, BLOCK), jnp.float32),
                   jax.ShapeDtypeStruct((2 * PLANE * LATE_PIECE, BLOCK), jnp.float32)),
        in_specs=[pl.BlockSpec(memory_space=pl.ANY)],
        out_specs=(pl.BlockSpec(memory_space=pl.ANY), pl.BlockSpec(memory_space=VMEM),
                   pl.BlockSpec(memory_space=VMEM)),
        scratch_shapes=[VMEM((ycount, NX, BLOCK), jnp.float32)] + scratch(EARLY_PIECE) + scratch(LATE_PIECE)
        + [dma, dma((2 * SPLIT,)), dma, dma((STEPS,)), dma((STEPS,))],
        compiler_params=pltpu.CompilerParams(collective_id=0, has_side_effects=True),
    )(snap)


def inverse_factor(a):
    n = a.shape[0]
    count = n // 8
    tiles = [a[8 * t:8 * t + 8, :] for t in range(count)]
    lane = lax.broadcasted_iota(jnp.int32, (8, n), 1)
    sub = lax.broadcasted_iota(jnp.int32, (8, n), 0)
    spread = lane - sub
    out = []
    for p in range(count):
        base = 8 * p
        own = tiles[p]
        cols = [jnp.take_along_axis(own, jnp.full((8, n), base + j, jnp.int32), axis=1) for j in range(8)]
        s = [[jnp.broadcast_to(cols[j][i:i + 1, :], (8, n)) for j in range(i + 1)] for i in range(8)]
        panel = (lane >= base) & (lane < base + 8)
        ready = jnp.where(panel, jnp.where(spread == base, 1.0, 0.0), own)
        rows = [jnp.broadcast_to(ready[j:j + 1, :], (8, n)) for j in range(8)]
        rinv, low = [], [[None] * 8 for _ in range(8)]
        for j in range(8):
            r = 1.0 / s[j][j]
            rinv.append(r)
            for i in range(j + 1, 8):
                low[i][j] = s[i][j] * r
                for k in range(j + 1, i + 1):
                    s[i][k] = s[i][k] - low[i][j] * s[k][j]
                rows[i] = rows[i] - low[i][j] * rows[j]
        merged, pivots = rows[0], s[0][0]
        for j in range(1, 8):
            merged = jnp.where(sub == j, rows[j], merged)
            pivots = jnp.where(sub == j, s[j][j], pivots)
        out.append(jnp.where(spread <= base, merged * lax.rsqrt(pivots), 0.0))
        if p + 1 == count:
            break
        solved = [rows[j] * rinv[j] for j in range(8)]
        for j in range(7, 0, -1):
            for i in range(j):
                solved[i] = solved[i] - low[j][i] * solved[j]
        rest = range(p + 1, count)
        acc = {t: jnp.where(panel, 0.0, tiles[t]) for t in rest}
        first = p + 1
        for j in range(8):
            acc[first] = acc[first] - jnp.broadcast_to(tiles[first][:, base + j:base + j + 1], (8, n)) * solved[j]
        for t in range(p + 2, count):
            for j in range(8):
                acc[t] = acc[t] - jnp.broadcast_to(tiles[t][:, base + j:base + j + 1], (8, n)) * solved[j]
        for t in rest:
            tiles[t] = acc[t]
    return jnp.concatenate(out, axis=0)


def basis_project_kernel(early_ref, late_ref, fib_hbm, core_ref, mine_ref, fib_ref, hi_ref, lo_ref,
                         m_ref, bt_ref, b_ref, sent_ref, fib_sem, send_sem, recv_sem):
    gx = lax.axis_index("gx")
    ycount = fib_ref.shape[0]
    ranks = core_ref.shape[0]
    peers = column_peers()
    barrier = pltpu.get_barrier_semaphore()
    for peer in peers:
        pl.semaphore_signal(barrier, inc=1, device_id={"gx": peer}, device_id_type=MESH)
    load = pltpu.make_async_copy(fib_hbm, fib_ref, fib_sem)
    load.start()

    nb = NX // BLOCK
    blocks, at = {}, 0
    for j in range(nb - 1):
        for i in range(j, nb - 1):
            blocks[i, j] = early_ref[pl.ds(at, BLOCK), :]
            at += BLOCK
    for i in range(nb):
        blocks[i, nb - 1] = late_ref[pl.ds(i * BLOCK, BLOCK), :]
    for i in range(nb):
        for j in range(nb):
            if (i, j) not in blocks:
                blocks[i, j] = blocks[j, i].T
    rows = [jnp.concatenate([blocks[i, j] for j in range(nb)], axis=1) for i in range(nb)]
    for i in range(nb):
        hi, lo = split(rows[i])
        hi_ref[pl.ds(i * BLOCK, BLOCK), :] = hi
        lo_ref[pl.ds(i * BLOCK, BLOCK), :] = lo
    per_block = RANK // (EARLY + LATE)
    for n in range(per_block):
        m_ref[pl.ds(n * (EARLY + LATE), EARLY), :] = rows[0][n * EARLY:(n + 1) * EARLY]
        m_ref[pl.ds(n * (EARLY + LATE) + EARLY, LATE), :] = rows[nb - 1][n * LATE:(n + 1) * LATE]

    def iterate(step, carry):
        m = split(m_ref[...])
        basis = dot_split(split(inverse_factor(dot_split(m, m, 1, 1))), m)
        bt_ref[...] = basis

        @pl.when(step < ITERS)
        def _():
            m_ref[...] = dot_split(split(basis), (hi_ref[...], lo_ref[...]))

        return carry

    lax.fori_loop(0, ITERS + 1, iterate, 0)
    basis = split(bt_ref[...])
    load.wait()
    pl.semaphore_wait(barrier, len(peers))

    def emit(y, carry):
        sent_ref[y] = dot_split(basis, split(fib_ref[y]))
        there = core_ref.at[:, gx * ycount + y]
        for peer in peers:
            pltpu.make_async_remote_copy(
                src_ref=sent_ref.at[y, pl.ds(pl.multiple_of(peer * ranks, ranks), ranks)],
                dst_ref=there, send_sem=send_sem, recv_sem=recv_sem,
                device_id={"gx": peer}, device_id_type=MESH).start()
        pltpu.make_async_copy(
            sent_ref.at[y, pl.ds(pl.multiple_of(gx * ranks, ranks), ranks)], there, recv_sem).start()
        return carry

    lax.fori_loop(0, ycount, emit, 0)
    b_ref[...] = bt_ref[...].T
    mine_ref[pl.ds(0, EARLY), :] = b_ref[pl.ds(pl.multiple_of(gx * EARLY, 8), EARLY), :]
    mine_ref[pl.ds(EARLY, LATE), :] = b_ref[pl.ds(pl.multiple_of(FIRST + gx * LATE, 8), LATE), :]
    done = sent_ref.at[:, pl.ds(0, RANK - RANK // GX)]
    pltpu.make_async_copy(done, done, send_sem).wait()
    pltpu.make_async_copy(core_ref, core_ref, recv_sem).wait()


def basis_project(fib, early, late):
    ycount = fib.shape[0]
    dma = pltpu.SemaphoreType.DMA
    return pl.pallas_call(
        basis_project_kernel,
        out_shape=(jax.ShapeDtypeStruct((RANK // GX, GX * ycount, BLOCK), jnp.float32),
                   jax.ShapeDtypeStruct((NX // GX, RANK), jnp.float32)),
        in_specs=[pl.BlockSpec(memory_space=VMEM)] * 2 + [pl.BlockSpec(memory_space=pl.ANY)],
        out_specs=(pl.BlockSpec(memory_space=pl.ANY), pl.BlockSpec(memory_space=VMEM)),
        scratch_shapes=[VMEM((ycount, NX, BLOCK), jnp.float32),
                        VMEM((NX, NX), jnp.bfloat16), VMEM((NX, NX), jnp.bfloat16),
                        VMEM((RANK, NX), jnp.float32), VMEM((RANK, NX), jnp.float32),
                        VMEM((NX, RANK), jnp.float32), VMEM((ycount, RANK, BLOCK), jnp.float32),
                        dma, dma, dma],
        compiler_params=pltpu.CompilerParams(collective_id=1, has_side_effects=True),
    )(early, late, fib)


def finish_kernel(core_ref, mine_ref, core_out, mine_out):
    core_out[...] = core_ref[...]
    mine_out[...] = mine_ref[...]


def finish(core, mine):
    return pl.pallas_call(
        finish_kernel,
        out_shape=(jax.ShapeDtypeStruct(core.shape, core.dtype), jax.ShapeDtypeStruct(mine.shape, mine.dtype)),
        in_specs=[pl.BlockSpec(memory_space=VMEM)] * 2,
        out_specs=(pl.BlockSpec(memory_space=VMEM),) * 2,
    )(core, mine)


def local(snapshot):
    fib, early, late = gather_gram(snapshot)
    core, mine = basis_project(fib, early, late)
    core, mine = finish(core, mine)
    return (mine, core)


def solution(mesh):
    in_specs = (P("gx", "gy", "gz"),)
    out_specs = (P("gx", None), P("gx", "gy", "gz"))
    return jax.shard_map(local, mesh=mesh, in_specs=in_specs, out_specs=out_specs, check_vma=False)
```
